32 devices in a mesh: node: 8 (over z, x), mp: 4 (over y, core).
Axes of the slice: x: 2, y: 2, z: 4, core: 2. Of those that a mesh axis runs over, the one named last changes fastest.
Arguments:
- stored_features: float32 [16384, 1024], P('node', 'mp'), may hold values from -6 to 6
- vertex_row_index: int32 [16384], P('node'), may hold values from 0 to 511
- neighbors: int32 [2, 16384, 16], P(None, 'node'), may hold values from 0 to 511
- counts: int32 [2, 16384], P(None, 'node'), may hold values from 1 to 16
- self_w1: float32 [1024, 256], P('mp'), may hold values from -0.1875 to 0.1875
- neigh_w1: float32 [1024, 256], P('mp'), may hold values from -0.1875 to 0.1875
- self_w2: float32 [256, 256], replicated, may hold values from -0.375 to 0.375
- neigh_w2: float32 [256, 256], replicated, may hold values from -0.375 to 0.375
- upstream: float32 [32, 512, 256], P('node', 'mp'), may hold values from -6 to 6
Outputs:
- layer_out: float32 [32, 512, 256], P('node', 'mp')
- grad_self1: float32 [1024, 256], P('mp')
- grad_neigh1: float32 [1024, 256], P('mp')
- grad_self2: float32 [256, 256], replicated
- grad_neigh2: float32 [256, 256], replicated
The draws below stay inside these ranges and needn't reach their ends.
Inputs may be any that keep to these rules, and one draw needn't show every extreme that they name: Only the first counts[l, r] slots of neighbors[l, r] are used; neighbour and stored-row numbers refer to the node's own subgraph.
All inputs are finite; a program needn't handle non-finite values.
Results may differ from the reference program's by a relative error of at most 0.003.
Values sent between devices are 32-bit elements; how exact they have to be, the bound alone decides.
A program may use at most 64 MiB of HBM per device.

```python
import math
import jax
import jax.numpy as jnp
import numpy as np
from jax import lax

F = 1024
H = 256
K = 16
NB = 512
GRAPHS = 32
NODES = 16384


def place_ends(array, rng, smallest, high):
    longest = array.shape.index(max(array.shape))
    spots = []
    for shift in (0, 1):
        where = [jax.random.randint(jax.random.fold_in(rng, axis), (), 0, length) for axis, length in enumerate(array.shape)]
        where[longest] = (where[longest] + shift) % array.shape[longest]
        spots.append(tuple(where))
    return array.at[spots[0]].set(smallest).at[spots[1]].set(high)


def steps_of(own_key, shape, shards, least, top_value):
    def one(dim, parts):
        draws = jax.random.uniform(jax.random.fold_in(jax.random.fold_in(own_key, 6), dim), (parts,), jnp.float32, least / len(shards), top_value / len(shards))
        return jnp.repeat(jnp.exp(draws), shape[dim] // parts).reshape((-1,) + (1,) * (len(shape) - dim - 1))

    gain = one(*shards[0])
    for cut in shards[1:]:
        gain = gain * one(*cut)
    return gain


def cumulative_ranks(number_of, slope):
    loads = [(1 << 20) // math.isqrt(grade ** slope) + 1 for grade in range(1, number_of + 1)]
    width = 1 + sum(loads) // (1 << 30)
    return np.cumsum(np.array([max(1, weight // width) for weight in loads]))


def ranked_ids(rng, extent, count, lean):
    listing = cumulative_ranks(count, lean)
    ticket = jax.random.randint(jax.random.fold_in(rng, 1), extent, 0, int(listing[count - 1]))
    standing = jnp.searchsorted(jnp.asarray(listing, jnp.int32), ticket, side="right")
    return jax.random.permutation(jax.random.fold_in(rng, 2), count)[standing].astype(jnp.int32)


def gaussian(key, dims, width, limit, shards=(), kind=jnp.bfloat16):
    loudness = steps_of(key, dims, shards, -0.22, 0.18) if shards else 1.0
    drawn = jax.random.normal(key, dims, jnp.float32) * width * loudness
    return jnp.minimum(jnp.maximum(drawn, -limit), limit).astype(kind)


def setup_inputs(seed: int = 0) -> dict:
    keys = jax.random.split(jax.random.key(seed), 10)
    return {
        "stored_features": gaussian(keys[0], (NODES, F), 1.0, 6.0, ((0, 8), (1, 4)), jnp.float32),
        "vertex_row_index": place_ends(jax.random.randint(keys[1], (NODES,), 0, NB), jax.random.fold_in(keys[1], 1), 0, NB - 1).astype(jnp.int32),
        "neighbors": place_ends(ranked_ids(keys[2], (2, NODES, K), NB, 2), jax.random.fold_in(keys[2], 3), 0, NB - 1).astype(jnp.int32),
        "counts": place_ends(jax.random.randint(keys[3], (2, NODES), 1, K + 1), jax.random.fold_in(keys[3], 1), 1, K).astype(jnp.int32),
        "self_w1": gaussian(keys[4], (F, H), F ** -0.5, 0.1875, ((0, 4),), jnp.float32),
        "neigh_w1": gaussian(keys[5], (F, H), F ** -0.5, 0.1875, ((0, 4),), jnp.float32),
        "self_w2": gaussian(keys[6], (H, H), H ** -0.5, 0.375, (), jnp.float32),
        "neigh_w2": gaussian(keys[7], (H, H), H ** -0.5, 0.375, (), jnp.float32),
        "upstream": gaussian(keys[8], (GRAPHS, NB, H), 1.0, 6.0, ((0, 8), (1, 4)), jnp.float32),
    }


epsilon = 1e-05
precise = lax.Precision.HIGHEST

def neighbor_mean(source_rows, neighbor_ids, row_counts):
    picked = jnp.take(source_rows, neighbor_ids, axis=0)
    slot_ids = jnp.arange(neighbor_ids.shape[1], dtype=jnp.int32)
    row_mask = (slot_ids[None, :] < row_counts[:, None]).astype(jnp.float32)
    summed = lax.optimization_barrier(jnp.sum(picked * row_mask[:, :, None], axis=1))
    return summed / row_counts[:, None].astype(jnp.float32)

def normed(pre_act):
    activated = jax.nn.relu(pre_act)
    return activated * lax.rsqrt(lax.optimization_barrier(jnp.mean(activated * activated, axis=1, keepdims=True)) + epsilon)

def block_forward(weights, store_rows, node_rows, neighbor_ids, row_counts):
    self_one, neigh_one, self_two, neigh_two = weights
    features = jnp.take(store_rows, node_rows, axis=0)
    agg_zero = neighbor_mean(features, neighbor_ids[0], row_counts[0])
    hidden = normed(jnp.dot(features, self_one, precision=precise) + jnp.dot(agg_zero, neigh_one, precision=precise))
    agg_one = neighbor_mean(hidden, neighbor_ids[1], row_counts[1])
    return jnp.dot(hidden, self_two, precision=precise) + jnp.dot(agg_one, neigh_two, precision=precise)

def reference(stored_features, vertex_row_index, neighbors, counts, self_w1, neigh_w1, self_w2, neigh_w2, upstream):
    gradient_scale = 1.0 / math.sqrt(NODES)
    stores = stored_features.reshape(GRAPHS, NB, F)
    vertex_blocks = vertex_row_index.reshape(GRAPHS, NB)
    neighbor_blocks = jnp.transpose(neighbors.reshape(2, GRAPHS, NB, K), (1, 0, 2, 3))
    block_count = jnp.transpose(counts.reshape(2, GRAPHS, NB), (1, 0, 2))
    cotangents = upstream * gradient_scale
    weights = (self_w1, neigh_w1, self_w2, neigh_w2)

    def per_block(packed):
        store_rows, node_rows, neighbor_ids, row_counts, cotangent = packed

        def forward(params):
            return block_forward(params, store_rows, node_rows, neighbor_ids, row_counts)
        block_out, pullback = jax.vjp(forward, weights)
        grad_sets, = pullback(cotangent)
        return (block_out, grad_sets)
    outputs, grad_sets = lax.map(per_block, (stores, vertex_blocks, neighbor_blocks, block_count, cotangents))
    return (outputs, lax.optimization_barrier(jnp.sum(grad_sets[0], axis=0)), lax.optimization_barrier(jnp.sum(grad_sets[1], axis=0)), lax.optimization_barrier(jnp.sum(grad_sets[2], axis=0)), lax.optimization_barrier(jnp.sum(grad_sets[3], axis=0)))
```

```python
import functools
import math

import jax
import jax.numpy as jnp
from jax import lax
from jax.experimental import pallas as pl
from jax.experimental.pallas import tpu as pltpu
from jax.sharding import PartitionSpec as P

epsilon = 1e-05
precise = lax.Precision.HIGHEST


def adjacency(neighbor_ids, row_counts, width):
    row_total = neighbor_ids.shape[0]
    slot_positions = neighbor_ids.shape[1]
    tile_rows = min(128, row_total)
    tiles = row_total // tile_rows
    column_ids = jnp.arange(width, dtype=jnp.int32)
    slot_ids = jnp.arange(slot_positions, dtype=jnp.int32)
    slot_weight = (slot_ids[None, :] < row_counts[:, None]).astype(jnp.float32) / row_counts[
        :, None
    ].astype(jnp.float32)

    def one_tile(packed):
        tile_ids, tile_weight = packed
        hits = (tile_ids[:, :, None] == column_ids[None, None, :]).astype(jnp.float32)
        return jnp.sum(hits * tile_weight[:, :, None], axis=1)

    tiled = lax.map(
        one_tile,
        (
            neighbor_ids.reshape(tiles, tile_rows, slot_positions),
            slot_weight.reshape(tiles, tile_rows, slot_positions),
        ),
    )
    return tiled.reshape(row_total, width)


def normed_parts(pre_act):
    activated = jnp.maximum(pre_act, 0.0)
    inverse = lax.rsqrt(jnp.mean(activated * activated, axis=1, keepdims=True) + epsilon)
    return (activated * inverse, activated, inverse)


def norm_backward(hidden_grad, activated, inverse, pre_act):
    inner_sum = jnp.mean(hidden_grad * activated, axis=1, keepdims=True)
    act_grad = inverse * hidden_grad - activated * (inverse * inverse * inverse) * inner_sum
    return jnp.where(pre_act > 0, act_grad, 0.0)


def body(
    stored_features,
    vertex_row_index,
    neighbors,
    counts,
    self_w1,
    neigh_w1,
    self_w2,
    neigh_w2,
    upstream,
):
    mp_index = lax.axis_index("mp")
    sampled_graphs = upstream.shape[0]
    own_rows = upstream.shape[1]
    row_grand_total = vertex_row_index.shape[0] // sampled_graphs
    column_total = stored_features.shape[1]
    slot_positions = neighbors.shape[2]
    gradient_scale = 1.0 / math.sqrt(row_grand_total * sampled_graphs * lax.axis_size("node"))
    first_row = mp_index * own_rows
    stored_blocks = stored_features.reshape(sampled_graphs, row_grand_total, column_total)
    vertex_blocks = vertex_row_index.reshape(sampled_graphs, row_grand_total)
    neighbor_blocks = jnp.transpose(
        neighbors.reshape(2, sampled_graphs, row_grand_total, slot_positions), (1, 0, 2, 3)
    )
    block_count = jnp.transpose(counts.reshape(2, sampled_graphs, row_grand_total), (1, 0, 2))

    def one_graph(carry, packed):
        store_rows, node_rows, neighbor_ids, row_counts, cotangent = packed
        features = jnp.take(store_rows, node_rows, axis=0)
        adj_zero = adjacency(neighbor_ids[0], row_counts[0], row_grand_total)
        agg_zero = jnp.dot(adj_zero, features, precision=precise)
        own_ids = lax.dynamic_slice_in_dim(neighbor_ids[1], first_row, own_rows, 0)
        own_counts = lax.dynamic_slice_in_dim(row_counts[1], first_row, own_rows, 0)
        adj_own = adjacency(own_ids, own_counts, row_grand_total)
        scaled = cotangent * gradient_scale
        back_neigh = jnp.dot(scaled, neigh_w2.T, precision=precise)
        back_self = jnp.dot(scaled, self_w2.T, precision=precise)
        contrib = lax.dot_general(adj_own, back_neigh, (((0,), (0,)), ((), ())), precision=precise)
        rows_self = features
        rows_neigh = agg_zero
        pre_own = lax.psum_scatter(
            jnp.dot(rows_self, self_w1, precision=precise)
            + jnp.dot(rows_neigh, neigh_w1, precision=precise),
            "mp",
            scatter_dimension=0,
            tiled=True,
        )
        hidden_own, act_own, inverse_own = normed_parts(pre_own)
        hidden_all = lax.all_gather(hidden_own, "mp", axis=0, tiled=True)
        agg_one = jnp.dot(adj_own, hidden_all, precision=precise)
        hidden_grad = lax.psum_scatter(contrib, "mp", scatter_dimension=0, tiled=True) + back_self
        pre_grad = norm_backward(hidden_grad, act_own, inverse_own, pre_own)
        grad_piece = lax.all_gather(pre_grad, "mp", axis=0, tiled=True)
        rows_self = features
        rows_neigh = agg_zero
        step_self1 = carry[0] + jnp.dot(rows_self.T, grad_piece, precision=precise)
        step_neigh1 = carry[1] + jnp.dot(rows_neigh.T, grad_piece, precision=precise)
        graph_out = jnp.dot(hidden_own, self_w2, precision=precise) + jnp.dot(
            agg_one, neigh_w2, precision=precise
        )
        step_self2 = carry[2] + jnp.dot(hidden_own.T, scaled, precision=precise)
        step_neigh2 = carry[3] + jnp.dot(agg_one.T, scaled, precision=precise)
        return ((step_self1, step_neigh1, step_self2, step_neigh2), graph_out)

    zero_first = jnp.zeros(self_w1.shape, jnp.float32)
    zero_second = jnp.zeros(self_w2.shape, jnp.float32)
    totals, layer_out = lax.scan(
        one_graph,
        (zero_first, zero_first, zero_second, zero_second),
        (stored_blocks, vertex_blocks, neighbor_blocks, block_count, upstream),
    )
    grad_self1, grad_neigh1, grad_self2, grad_neigh2 = totals
    grad_self1, grad_neigh1, grad_self2, grad_neigh2 = lax.psum(
        (grad_self1, grad_neigh1, grad_self2, grad_neigh2), "node"
    )
    grad_self2, grad_neigh2 = lax.psum((grad_self2, grad_neigh2), "mp")
    return (layer_out, grad_self1, grad_neigh1, grad_self2, grad_neigh2)


f32 = jnp.float32
bf16 = jnp.bfloat16


def halves(value):
    high = value.astype(bf16)
    return high, (value - high.astype(f32)).astype(bf16)


def thirds(value):
    high = value.astype(bf16)
    rest = value - high.astype(f32)
    middle = rest.astype(bf16)
    return high, middle, (rest - middle.astype(f32)).astype(bf16)


def mul(left, right, dims=((1,), (0,))):
    return lax.dot_general(left, right, (dims, ((), ())), preferred_element_type=f32)


def mul3(left, right, dims=((1,), (0,))):
    return (
        mul(left[0], right[0], dims) + mul(left[1], right[0], dims) + mul(left[0], right[1], dims)
    )


def mul6(left, right):
    small = mul(left[2], right[0]) + mul(left[0], right[2]) + mul(left[1], right[1])
    return mul(left[0], right[0]) + (mul(left[0], right[1]) + mul(left[1], right[0]) + small)


def thin(value):
    return value[0] + value[1] + value[2]


def fused_kernel(
    slots,
    scale,
    store_h,
    nbr_h,
    vertex_h,
    counts_h,
    s1_h,
    n1_h,
    s2_h,
    n2_h,
    up_h,
    out_ref,
    g1_ref,
    g2_ref,
    store,
    nbr,
    vertex,
    counts,
    w1f,
    w2f,
    upg,
    grid,
    adj_even,
    adj_odd,
    hot_even,
    hot_odd,
    rec_t,
    rec,
    part,
    pin,
    psum,
    near,
    far,
    pg,
    xh,
    xl,
    xt,
    wh,
    wl,
    wt,
    hid,
    hg,
    g1acc,
    g2acc,
    g2p,
    g2y,
    q2,
    outg,
    xin,
    half,
    zin,
    mid,
    xin2,
    half2,
    zin2,
    mid2,
    load_sems,
    send_sems,
    recv_sems,
):
    rows, width = upg.shape
    own = up_h.shape[1]
    cols = store_h.shape[1]
    node = lax.axis_index("node")
    member = lax.axis_index("mp")
    zc, xc = node // 2, node % 2
    yc, cc = member // 2, member % 2
    partner = yc * 2 + (1 - cc)
    across = (1 - yc) * 2 + cc
    diagonal = (1 - yc) * 2 + (1 - cc)
    peers = (partner, across, diagonal)
    x_peer = zc * 2 + (1 - xc)
    z_pair = (zc + 1 - 2 * (zc % 2)) * 2 + xc
    z_mate = (3 - zc) * 2 + xc
    inner = jnp.logical_or(zc == 1, zc == 2)
    outer = jnp.logical_or(zc == 0, zc == 3)
    graphs = ((1 - yc) * 2, (1 - yc) * 2 + 1, partner, member)

    def target(node_id, member_id):
        return dict(device_id=(node_id, member_id), device_id_type=pl.DeviceIdType.MESH)

    counter = [0]

    def take(n):
        k = counter[0]
        counter[0] += n
        return k

    def copy(source, dest, node_id, member_id, send=None, recv=None):
        k = take(1) if send is None else 0
        return pltpu.make_async_remote_copy(
            src_ref=source,
            dst_ref=dest,
            send_sem=send_sems.at[k if send is None else send],
            recv_sem=recv_sems.at[k if recv is None else recv],
            **target(node_id, member_id),
        )

    def block(index, size):
        return pl.ds(pl.multiple_of(index * size, size), size)

    loads = [0]

    def load(source, dest):
        k = loads[0]
        loads[0] += 1
        one = pltpu.make_async_copy(source, dest, load_sems.at[k])
        one.start()
        return one

    barrier = pltpu.get_barrier_semaphore()
    for p in peers:
        pl.semaphore_signal(barrier, inc=1, **target(node, p))
    pl.semaphore_signal(barrier, inc=1, **target(x_peer, member))
    pl.semaphore_signal(barrier, inc=1, **target(z_pair, member))
    pl.semaphore_signal(barrier, inc=1, **target(z_mate, member))

    id_loads = [load(nbr_h, nbr), load(vertex_h, vertex), load(counts_h, counts)]
    store_loads = [load(store_h.at[block(graphs[0], rows)], store.at[0])]
    w1_loads = [load(s1_h, w1f.at[0]), load(n1_h, w1f.at[1])]
    for s in range(1, 4):
        store_loads.append(load(store_h.at[block(graphs[s], rows)], store.at[s]))
    w2_loads = [load(s2_h, w2f.at[0]), load(n2_h, w2f.at[1])]
    up_load = load(up_h.at[member], upg.at[block(member, own)])

    packs = rows // 16
    middle = rows // 2
    spot = lax.broadcasted_iota(jnp.int32, (packs, 16, 128), 0) * 16
    spot = spot + lax.broadcasted_iota(jnp.int32, (packs, 16, 128), 1) - middle
    grid[...] = spot.astype(f32).astype(bf16)
    rec_t[...] = jnp.ones_like(rec_t)
    one_b, none_b = jnp.ones((), bf16), jnp.zeros((), bf16)
    slot = lax.broadcasted_iota(jnp.int32, (slots, 128), 0)
    group = 8

    def pieces(adj, hot, layer, graph):
        todo = []
        for c in range(rows // 128):
            lane = pl.ds(pl.multiple_of(graph * rows + c * 128, 128), 128)
            to = pl.ds(c * 128, 128)

            def prepare(lane=lane):
                used = slot < counts[layer : layer + 1, lane]
                ids = jnp.where(used, nbr[layer, :, lane], 4 * rows)
                ids = (ids - middle).astype(f32)
                keys = [
                    jnp.broadcast_to(ids[k : k + 1], (16, 128)).astype(bf16) for k in range(slots)
                ]
                if hot is None:
                    return keys
                at = (vertex[0:1, lane] - middle).astype(f32)
                return keys + [jnp.broadcast_to(at, (16, 128)).astype(bf16)]

            kept = []
            for j in range(packs // group):

                def unit(j=j, prepare=prepare, kept=kept, to=to):
                    if not kept:
                        kept.append(prepare())
                    keys = kept[0]
                    span = pl.ds(j * group, group)
                    lanes = grid[span]
                    total = jnp.where(keys[0][None] == lanes, one_b, none_b)
                    for k in range(1, slots):
                        total = total + jnp.where(keys[k][None] == lanes, one_b, none_b)
                    adj[span, :, to] = total
                    if hot is not None:
                        hot[span, :, to] = jnp.where(keys[slots][None] == lanes, one_b, none_b)

                todo.append(unit)
        return todo

    def square(ref):
        return ref[...].reshape(rows, rows)

    tn = ((0,), (0,))
    nt = ((1,), (1,))

    for one in id_loads:
        one.wait()
    with jax.named_scope("first_build"):
        for unit in pieces(adj_even, hot_even, 0, graphs[0]):
            unit()
        for s in range(4):
            rec_t[s : s + 1] = 1.0 / counts[0:1, block(graphs[s], rows)].astype(f32)
        rec_t[4:5] = 1.0 / counts[1:2, block(member, rows)].astype(f32)
        rec[...] = jnp.transpose(rec_t[...])

    with jax.named_scope("barrier"):
        pl.semaphore_wait(barrier, 6)
    up_copies = [copy(up_h.at[p], upg.at[block(member, own)], node, p) for p in peers]
    for one in up_copies:
        one.start()
    for one in w1_loads:
        one.wait()
    wh[:cols], wl[:cols], wt[:cols] = thirds(w1f[0])
    wh[cols:], wl[cols:], wt[cols:] = thirds(w1f[1])

    side = rows // 2
    pin_copies = [
        copy(part.at[s, block(1 - cc, side)], pin.at[s], node, partner) for s in range(2)
    ]
    far_send, far_recv = take(2), 0
    far_recv = far_send
    far_copies = [
        copy(
            psum.at[s],
            far.at[block(cc, side)],
            node,
            (1 - yc) * 2 + s,
            send=far_send + s,
            recv=far_recv + cc,
        )
        for s in range(2)
    ]
    far_waits = [
        copy(
            psum.at[i],
            far.at[pl.ds(i * side, side)],
            node,
            across,
            send=far_send + i,
            recv=far_recv + i,
        )
        for i in range(2)
    ]
    near_copy = copy(part.at[2], near, node, partner)

    def pass_on(s):
        pin_copies[s].wait_recv()
        psum[s] = part[s, block(cc, side)] + pin[s]
        far_copies[s].start()

    tiles = rows // 128
    for s in range(4):
        adj, hot = (adj_even, hot_even) if s % 2 == 0 else (adj_odd, hot_odd)
        adj_next, hot_next = (adj_odd, hot_odd) if s % 2 == 0 else (adj_even, hot_even)
        with jax.named_scope(f"graph{s}"):
            store_loads[s].wait()
            if s < 3:
                todo = pieces(adj_next, hot_next, 0, graphs[s + 1])
            else:
                todo = pieces(adj_next, None, 1, member)
            per = -(-len(todo) // (2 * tiles))

            def some():
                for _ in range(per):
                    if todo:
                        todo.pop(0)()

            kept = jnp.concatenate(thirds(store[s]), axis=1)
            for t in range(tiles):
                span = pl.ds(t * 128, 128)
                pick = hot[:, :, span].reshape(rows, 128)
                found = mul(pick, kept, tn)
                xh[s, span, :cols] = found[:, :cols].astype(bf16)
                xl[s, span, :cols] = found[:, cols : 2 * cols].astype(bf16)
                xt[span, :cols] = found[:, 2 * cols :].astype(bf16)
                some()
            source = jnp.concatenate([xt[:, :cols], xl[s, :, :cols], xh[s, :, :cols]], axis=1)
            for t in range(tiles):
                span = pl.ds(t * 128, 128)
                pick = adj[:, :, span].reshape(rows, 128)
                agg = mul(pick, source, tn)
                agg = agg[:, :cols] + agg[:, cols : 2 * cols] + agg[:, 2 * cols :]
                ah, al, at = thirds(agg * rec[span, s : s + 1])
                xh[s, span, cols:] = ah
                xl[s, span, cols:] = al
                xt[span, cols:] = at
                part[s, span] = mul6(
                    (xh[s, span], xl[s, span], xt[span]), (wh[...], wl[...], wt[...])
                )
                some()
        if s < 2:
            pin_copies[s].start()
        if s == 2:
            near_copy.start()
        if s == 1:
            pass_on(0)
        if s == 2:
            pass_on(1)

    shrink = rec[:, 4:5]
    with jax.named_scope("back"):
        for one in w2_loads:
            one.wait()
        up_load.wait()
        for one in up_copies:
            one.wait_recv()
        scaled = halves(upg[...] * scale)
        w2s = halves(w2f[0])
        w2n = halves(w2f[1])
        back = halves(mul3(scaled, w2n, nt) * shrink)
        adj = square(adj_even)
        hg[...] = mul3(scaled, w2s, nt) + mul(adj, back[0]) + mul(adj, back[1])

    pg_partner = copy(pg.at[3], pg.at[2], node, partner)
    parts = [pl.ds(i * own, own) for i in range(4)]
    pg_across = [copy(pg.at[3, r], pg.at[cc, r], node, across) for r in parts]
    pg_forward = [copy(pg.at[cc, r], pg.at[cc, r], node, partner) for r in parts]
    with jax.named_scope("norm"):
        near_copy.wait_recv()
        for i in range(2):
            far_waits[i].wait_recv()
            span = pl.ds(i * side, side)
            pre = part[3, span] + near[span] + far[span]
            hidden, activated, inverse = normed_parts(pre)
            hid[span] = hidden
            pg[3, span] = norm_backward(hg[span], activated, inverse, pre)
            for one in pg_across[2 * i : 2 * i + 2]:
                one.start()
        pg_partner.start()

    with jax.named_scope("second_gradients"):
        hidden = halves(hid[...])
        adj = square(adj_even)
        agg_one = halves((mul(adj, hidden[0], tn) + mul(adj, hidden[1], tn)) * shrink)
        scaled = halves(upg[...] * scale)
        g2acc[0] = mul3(hidden, scaled, tn)
        g2acc[1] = mul3(agg_one, scaled, tn)
        g2_partner = copy(g2acc.at[1 - cc], g2p, node, partner)
        g2_partner.start()
    with jax.named_scope("output"):
        w2s = halves(w2f[0])
        w2n = halves(w2f[1])
        outg[...] = mul3(hidden, w2s) + mul3(agg_one, w2n)
    fourth = q2.shape[0]
    g2_partner.wait_recv()
    g2acc[cc] = g2acc[cc] + g2p[...]
    g2_across = copy(g2acc.at[cc, block(1 - yc, fourth)], g2y, node, across)
    g2_across.start()
    out_copies = [copy(outg.at[block(p, own)], out_ref.at[member], node, p) for p in peers]
    for one in out_copies[1:] + out_copies[:1]:
        one.start()
    out_ref[member] = outg[block(member, own)]

    def both(k):
        return xh[k], xl[k]

    with jax.named_scope("early_gradients"):
        g1acc[...] = mul3(both(3), halves(pg[3]), tn)
        pg_partner.wait_recv()
        g1acc[...] += mul3(both(2), halves(pg[2]), tn)
    with jax.named_scope("across_wait"):
        for one, onward in zip(pg_across, pg_forward):
            one.wait_recv()
            onward.start()
    with jax.named_scope("late_gradients"):
        g1acc[...] += mul3(both(cc), halves(pg[cc]), tn)
        for one in pg_forward:
            one.wait_recv()

    chunk = 64
    sets = []
    chunks = g1acc.shape[0] // chunk
    base2 = pl.multiple_of(cc * 2 * fourth + yc * fourth, fourth)
    plan = [(g1acc, e * chunk, e * chunk, chunk, g1_ref, e, (xin, half, zin, mid)) for e in range(chunks)]
    plan.append((q2, 0, base2, fourth, g2_ref, 0, (xin2, half2, zin2, mid2)))
    for full, base, to, size, result, i, bufs in plan:
        size = size // 2
        x_in, x_sum, z_in, m_in = [b.at[i] for b in bufs]
        away = pl.ds(pl.multiple_of(base + (1 - xc) * size, size), size)
        home = pl.ds(pl.multiple_of(base + xc * size, size), size)
        mine = pl.ds(pl.multiple_of(to + xc * size, size), size)
        sets.append(
            dict(
                full=full,
                home=home,
                mine=mine,
                result=result,
                bufs=(x_in, x_sum, z_in, m_in),
                x=copy(full.at[away], x_in, x_peer, member),
                z=copy(x_sum, z_in, z_pair, member),
                m=copy(x_sum, m_in, z_mate, member),
                o=copy(result.at[mine], result.at[mine], z_pair, member),
                e=copy(result.at[mine], result.at[mine], x_peer, member),
            )
        )

    def stage_x(one):
        x_in, x_sum, z_in, m_in = one["bufs"]
        one["x"].wait_recv()
        x_sum[...] = one["full"][one["home"]] + x_in[...]

        @pl.when(outer)
        def _():
            one["z"].start()

    def stage_z(one):
        x_in, x_sum, z_in, m_in = one["bufs"]

        @pl.when(inner)
        def _():
            one["z"].wait_recv()
            x_sum[...] = x_sum[...] + z_in[...]
            one["m"].start()

    def stage_m(one):
        x_in, x_sum, z_in, m_in = one["bufs"]

        @pl.when(inner)
        def _():
            one["m"].wait_recv()
            one["result"][one["mine"]] = x_sum[...] + m_in[...]
            one["o"].start()
            one["e"].start()

    def stage_o(one):
        @pl.when(outer)
        def _():
            one["o"].wait_recv()
            one["e"].start()

    def finish(one):
        for key in one["waits"]:
            one[key].wait_recv()

    second = sets[-1]
    with jax.named_scope("last_gradients"):
        other = 1 - cc
        moved = halves(pg[other])
        for c in range(g1acc.shape[0] // 128):
            span = pl.ds(c * 128, 128)
            picked = (xh[other, :, span], xl[other, :, span])
            g1acc[span] += mul3(picked, moved, tn)
            for e in range(c * (128 // chunk), (c + 1) * (128 // chunk)):
                sets[e]["x"].start()

    here = block(cc * 2 + yc, fourth)
    there = block(cc * 2 + 1 - yc, fourth)
    g2_near = copy(g2_ref.at[here], g2_ref.at[here], node, partner)
    g2_far = copy(g2_ref.at[here], g2_ref.at[here], node, across)
    g2_onward = copy(g2_ref.at[there], g2_ref.at[there], node, partner)

    lag = 3
    order = list(range(chunks))
    order.insert(5, chunks)
    with jax.named_scope("reduce"):
        for t in range(len(order) + 4 * lag):
            def at(delay):
                return sets[order[t - delay]] if 0 <= t - delay < len(order) else None
            if t == 2:
                g2_across.wait_recv()
                q2[...] = g2acc[cc, block(yc, fourth)] + g2y[...]
                second["x"].start()
            for delay, stage in ((0, stage_x), (lag, stage_z), (2 * lag, stage_m), (3 * lag, stage_o)):
                if at(delay) is not None:
                    stage(at(delay))
            if at(4 * lag) is not None:
                at(4 * lag)["e"].wait_recv()
                if at(4 * lag) is second:
                    g2_far.start()
                    g2_near.start()
    with jax.named_scope("g2_spread"):
        g2_far.wait_recv()
        g2_onward.start()
        g2_near.wait_recv()
        g2_onward.wait_recv()

    with jax.named_scope("drain"):
        for one in up_copies + pin_copies + [near_copy, pg_partner] + pg_across + pg_forward:
            one.wait_send()
        for one in far_copies + [g2_partner, g2_across, g2_near, g2_far, g2_onward]:
            one.wait_send()
        for one in out_copies:
            one.wait()
        for one in sets:
            one["x"].wait_send()
            one["e"].wait_send()

        @pl.when(outer)
        def _():
            for one in sets:
                one["z"].wait_send()

        @pl.when(inner)
        def _():
            for one in sets:
                one["m"].wait_send()
                one["o"].wait_send()


def place_kernel(out_ref, g1_ref, g2_ref, out, gs1, gn1, gs2, gn2, sems):
    cols, width = gs1.shape[0], gs2.shape[0]
    pairs = [
        (out_ref, out),
        (g1_ref.at[pl.ds(0, cols)], gs1),
        (g1_ref.at[pl.ds(cols, cols)], gn1),
        (g2_ref.at[pl.ds(0, width)], gs2),
        (g2_ref.at[pl.ds(width, width)], gn2),
    ]
    copies = [pltpu.make_async_copy(a, b, sems.at[i]) for i, (a, b) in enumerate(pairs)]
    for one in copies:
        one.start()
    for one in copies:
        one.wait()


def fused(mesh_node):
    def run(stored, vertex, neighbors, counts, self_w1, neigh_w1, self_w2, neigh_w2, upstream):
        graphs, own, width = upstream.shape
        rows = vertex.shape[0] // graphs
        slots = neighbors.shape[2]
        cols = stored.shape[1]
        total = vertex.shape[0]
        turned = jnp.transpose(neighbors, (0, 2, 1))
        scale = 1.0 / math.sqrt(total * mesh_node)
        wide = 2 * cols
        fourth = 2 * width // 4
        chunks = wide // 64
        vm = pltpu.VMEM
        scratch = [
            vm((4, rows, cols), f32),
            vm(turned.shape, jnp.int32),
            vm((1, total), jnp.int32),
            vm(counts.shape, jnp.int32),
            vm((2, cols, width), f32),
            vm((2, width, width), f32),
            vm((rows, width), f32),
            vm((rows // 16, 16, 128), bf16),
            vm((rows // 16, 16, rows), bf16),
            vm((rows // 16, 16, rows), bf16),
            vm((rows // 16, 16, rows), bf16),
            vm((rows // 16, 16, rows), bf16),
            vm((128, rows), f32),
            vm((rows, 128), f32),
            vm((4, rows, width), f32),
            vm((2, rows // 2, width), f32),
            vm((2, rows // 2, width), f32),
            vm((rows, width), f32),
            vm((rows, width), f32),
            vm((4, rows, width), f32),
            vm((4, rows, wide), bf16),
            vm((4, rows, wide), bf16),
            vm((rows, wide), bf16),
            vm((wide, width), bf16),
            vm((wide, width), bf16),
            vm((wide, width), bf16),
            vm((rows, width), f32),
            vm((rows, width), f32),
            vm((wide, width), f32),
            vm((2, width, width), f32),
            vm((width, width), f32),
            vm((fourth, width), f32),
            vm((fourth, width), f32),
            vm((rows, width), f32),
        ]
        scratch += [vm((chunks, 32, width), f32) for _ in range(4)]
        scratch += [vm((1, fourth // 2, width), f32) for _ in range(4)]
        scratch += [
            pltpu.SemaphoreType.DMA((16,)),
            pltpu.SemaphoreType.DMA((40 + 5 * (chunks + 1),)),
            pltpu.SemaphoreType.DMA((40 + 5 * (chunks + 1),)),
        ]
        anywhere = pl.BlockSpec(memory_space=pl.ANY)
        fast = pl.BlockSpec(memory_space=pltpu.VMEM)
        held = pl.pallas_call(
            functools.partial(fused_kernel, slots, scale),
            out_shape=(
                pltpu.VMEM((graphs, own, width), f32),
                pltpu.VMEM((wide, width), f32),
                pltpu.VMEM((2 * width, width), f32),
            ),
            in_specs=[anywhere] * 9,
            out_specs=(fast,) * 3,
            scratch_shapes=scratch,
            compiler_params=pltpu.CompilerParams(
                collective_id=0, has_side_effects=True, vmem_limit_bytes=60 * 1024 * 1024
            ),
        )(stored, turned, vertex[None], counts, self_w1, neigh_w1, self_w2, neigh_w2, upstream)
        first = jax.ShapeDtypeStruct((cols, width), f32)
        later = jax.ShapeDtypeStruct((width, width), f32)
        return pl.pallas_call(
            place_kernel,
            out_shape=(jax.ShapeDtypeStruct((graphs, own, width), f32), first, first, later, later),
            in_specs=[anywhere] * 3,
            out_specs=(anywhere,) * 5,
            scratch_shapes=[pltpu.SemaphoreType.DMA((5,))],
        )(*[pltpu.with_memory_space_constraint(one, pltpu.VMEM) for one in held])

    return run


def fitted(mesh):
    node_total, members = mesh.shape["node"], mesh.shape["mp"]

    def run(*args):
        vertex, upstream, stored = args[1], args[8], args[0]
        graphs, own, width = upstream.shape
        fits = (
            members == 4
            and graphs == members
            and node_total == 8
            and own == 128
            and own * members * graphs == vertex.shape[0]
            and args[2].shape[2] % 8 == 0
            and width == 256
            and stored.shape[1] == width
        )
        return (fused(node_total) if fits else body)(*args)

    return run


def solution(mesh):
    placed = (
        P("node", "mp"),
        P("node"),
        P(None, "node", None),
        P(None, "node"),
        P("mp", None),
        P("mp", None),
        P(),
        P(),
        P("node", "mp", None),
    )
    return jax.shard_map(
        fitted(mesh),
        mesh=mesh,
        in_specs=placed,
        out_specs=(P("node", "mp", None), P("mp", None), P("mp", None), P(), P()),
        check_vma=False,
    )
```

```python
import functools
import math

import jax
import jax.numpy as jnp
from jax import lax
from jax.experimental import pallas as pl
from jax.experimental.pallas import tpu as pltpu
from jax.sharding import PartitionSpec as P

epsilon = 1e-05
precise = lax.Precision.HIGHEST


def adjacency(neighbor_ids, row_counts, width):
    row_total = neighbor_ids.shape[0]
    slot_positions = neighbor_ids.shape[1]
    tile_rows = min(128, row_total)
    tiles = row_total // tile_rows
    column_ids = jnp.arange(width, dtype=jnp.int32)
    slot_ids = jnp.arange(slot_positions, dtype=jnp.int32)
    slot_weight = (slot_ids[None, :] < row_counts[:, None]).astype(jnp.float32) / row_counts[
        :, None
    ].astype(jnp.float32)

    def one_tile(packed):
        tile_ids, tile_weight = packed
        hits = (tile_ids[:, :, None] == column_ids[None, None, :]).astype(jnp.float32)
        return jnp.sum(hits * tile_weight[:, :, None], axis=1)

    tiled = lax.map(
        one_tile,
        (
            neighbor_ids.reshape(tiles, tile_rows, slot_positions),
            slot_weight.reshape(tiles, tile_rows, slot_positions),
        ),
    )
    return tiled.reshape(row_total, width)


def normed_parts(pre_act):
    activated = jnp.maximum(pre_act, 0.0)
    inverse = lax.rsqrt(jnp.mean(activated * activated, axis=1, keepdims=True) + epsilon)
    return (activated * inverse, activated, inverse)


def norm_backward(hidden_grad, activated, inverse, pre_act):
    inner_sum = jnp.mean(hidden_grad * activated, axis=1, keepdims=True)
    act_grad = inverse * hidden_grad - activated * (inverse * inverse * inverse) * inner_sum
    return jnp.where(pre_act > 0, act_grad, 0.0)


def body(
    stored_features,
    vertex_row_index,
    neighbors,
    counts,
    self_w1,
    neigh_w1,
    self_w2,
    neigh_w2,
    upstream,
):
    mp_index = lax.axis_index("mp")
    sampled_graphs = upstream.shape[0]
    own_rows = upstream.shape[1]
    row_grand_total = vertex_row_index.shape[0] // sampled_graphs
    column_total = stored_features.shape[1]
    slot_positions = neighbors.shape[2]
    gradient_scale = 1.0 / math.sqrt(row_grand_total * sampled_graphs * lax.axis_size("node"))
    first_row = mp_index * own_rows
    stored_blocks = stored_features.reshape(sampled_graphs, row_grand_total, column_total)
    vertex_blocks = vertex_row_index.reshape(sampled_graphs, row_grand_total)
    neighbor_blocks = jnp.transpose(
        neighbors.reshape(2, sampled_graphs, row_grand_total, slot_positions), (1, 0, 2, 3)
    )
    block_count = jnp.transpose(counts.reshape(2, sampled_graphs, row_grand_total), (1, 0, 2))

    def one_graph(carry, packed):
        store_rows, node_rows, neighbor_ids, row_counts, cotangent = packed
        features = jnp.take(store_rows, node_rows, axis=0)
        adj_zero = adjacency(neighbor_ids[0], row_counts[0], row_grand_total)
        agg_zero = jnp.dot(adj_zero, features, precision=precise)
        own_ids = lax.dynamic_slice_in_dim(neighbor_ids[1], first_row, own_rows, 0)
        own_counts = lax.dynamic_slice_in_dim(row_counts[1], first_row, own_rows, 0)
        adj_own = adjacency(own_ids, own_counts, row_grand_total)
        scaled = cotangent * gradient_scale
        back_neigh = jnp.dot(scaled, neigh_w2.T, precision=precise)
        back_self = jnp.dot(scaled, self_w2.T, precision=precise)
        contrib = lax.dot_general(adj_own, back_neigh, (((0,), (0,)), ((), ())), precision=precise)
        rows_self = features
        rows_neigh = agg_zero
        pre_own = lax.psum_scatter(
            jnp.dot(rows_self, self_w1, precision=precise)
            + jnp.dot(rows_neigh, neigh_w1, precision=precise),
            "mp",
            scatter_dimension=0,
            tiled=True,
        )
        hidden_own, act_own, inverse_own = normed_parts(pre_own)
        hidden_all = lax.all_gather(hidden_own, "mp", axis=0, tiled=True)
        agg_one = jnp.dot(adj_own, hidden_all, precision=precise)
        hidden_grad = lax.psum_scatter(contrib, "mp", scatter_dimension=0, tiled=True) + back_self
        pre_grad = norm_backward(hidden_grad, act_own, inverse_own, pre_own)
        grad_piece = lax.all_gather(pre_grad, "mp", axis=0, tiled=True)
        rows_self = features
        rows_neigh = agg_zero
        step_self1 = carry[0] + jnp.dot(rows_self.T, grad_piece, precision=precise)
        step_neigh1 = carry[1] + jnp.dot(rows_neigh.T, grad_piece, precision=precise)
        graph_out = jnp.dot(hidden_own, self_w2, precision=precise) + jnp.dot(
            agg_one, neigh_w2, precision=precise
        )
        step_self2 = carry[2] + jnp.dot(hidden_own.T, scaled, precision=precise)
        step_neigh2 = carry[3] + jnp.dot(agg_one.T, scaled, precision=precise)
        return ((step_self1, step_neigh1, step_self2, step_neigh2), graph_out)

    zero_first = jnp.zeros(self_w1.shape, jnp.float32)
    zero_second = jnp.zeros(self_w2.shape, jnp.float32)
    totals, layer_out = lax.scan(
        one_graph,
        (zero_first, zero_first, zero_second, zero_second),
        (stored_blocks, vertex_blocks, neighbor_blocks, block_count, upstream),
    )
    grad_self1, grad_neigh1, grad_self2, grad_neigh2 = totals
    grad_self1, grad_neigh1, grad_self2, grad_neigh2 = lax.psum(
        (grad_self1, grad_neigh1, grad_self2, grad_neigh2), "node"
    )
    grad_self2, grad_neigh2 = lax.psum((grad_self2, grad_neigh2), "mp")
    return (layer_out, grad_self1, grad_neigh1, grad_self2, grad_neigh2)


f32 = jnp.float32
bf16 = jnp.bfloat16


def halves(value):
    high = value.astype(bf16)
    return high, (value - high.astype(f32)).astype(bf16)


def thirds(value):
    high = value.astype(bf16)
    rest = value - high.astype(f32)
    middle = rest.astype(bf16)
    return high, middle, (rest - middle.astype(f32)).astype(bf16)


def mul(left, right, dims=((1,), (0,))):
    return lax.dot_general(left, right, (dims, ((), ())), preferred_element_type=f32)


def mul3(left, right, dims=((1,), (0,))):
    return (
        mul(left[0], right[0], dims) + mul(left[1], right[0], dims) + mul(left[0], right[1], dims)
    )


def mul6(left, right):
    small = mul(left[2], right[0]) + mul(left[0], right[2]) + mul(left[1], right[1])
    return mul(left[0], right[0]) + (mul(left[0], right[1]) + mul(left[1], right[0]) + small)


def fused_kernel(
    slots,
    scale,
    store_h,
    nbr_h,
    vertex_h,
    counts_h,
    s1_h,
    n1_h,
    s2_h,
    n2_h,
    up_h,
    out_ref,
    g1_ref,
    g2_ref,
    store,
    nbr,
    vertex,
    counts,
    w1f,
    w2f,
    upg,
    grid,
    adj_even,
    adj_odd,
    hot_even,
    hot_odd,
    rec_t,
    rec,
    part,
    pin,
    psum,
    near,
    far,
    pg,
    xh,
    xl,
    xt,
    wh,
    wl,
    wt,
    hid,
    hg,
    g1acc,
    g2acc,
    g2p,
    outg,
    xin,
    half,
    zin,
    mid,
    xin2,
    half2,
    zin2,
    mid2,
    yin2,
    load_sems,
    send_sems,
    recv_sems,
):
    rows, width = upg.shape
    own = up_h.shape[1]
    cols = store_h.shape[1]
    node = lax.axis_index("node")
    member = lax.axis_index("mp")
    zc, xc = node // 2, node % 2
    yc, cc = member // 2, member % 2
    partner = yc * 2 + (1 - cc)
    across = (1 - yc) * 2 + cc
    diagonal = (1 - yc) * 2 + (1 - cc)
    peers = (partner, across, diagonal)
    x_peer = zc * 2 + (1 - xc)
    z_pair = (zc + 1 - 2 * (zc % 2)) * 2 + xc
    z_mate = (3 - zc) * 2 + xc
    inner = jnp.logical_or(zc == 1, zc == 2)
    outer = jnp.logical_or(zc == 0, zc == 3)
    graphs = ((1 - yc) * 2, (1 - yc) * 2 + 1, partner, member)

    def target(node_id, member_id):
        return dict(device_id=(node_id, member_id), device_id_type=pl.DeviceIdType.MESH)

    counter = [0]

    def take(n):
        k = counter[0]
        counter[0] += n
        return k

    def copy(source, dest, node_id, member_id, send=None, recv=None):
        k = take(1) if send is None else 0
        return pltpu.make_async_remote_copy(
            src_ref=source,
            dst_ref=dest,
            send_sem=send_sems.at[k if send is None else send],
            recv_sem=recv_sems.at[k if recv is None else recv],
            **target(node_id, member_id),
        )

    def block(index, size):
        return pl.ds(pl.multiple_of(index * size, size), size)

    loads = [0]

    def load(source, dest):
        k = loads[0]
        loads[0] += 1
        one = pltpu.make_async_copy(source, dest, load_sems.at[k])
        one.start()
        return one

    barrier = pltpu.get_barrier_semaphore()
    for p in peers:
        pl.semaphore_signal(barrier, inc=1, **target(node, p))
    pl.semaphore_signal(barrier, inc=1, **target(x_peer, member))
    pl.semaphore_signal(barrier, inc=1, **target(z_pair, member))
    pl.semaphore_signal(barrier, inc=1, **target(z_mate, member))
    z_cross = (zc + 1 - 2 * (zc % 2)) * 2 + (1 - xc)
    pl.semaphore_signal(barrier, inc=1, **target(z_cross, member))

    id_loads = [load(nbr_h, nbr), load(vertex_h, vertex), load(counts_h, counts)]
    store_loads = [load(store_h.at[block(graphs[0], rows)], store.at[0])]
    w1_loads = [load(s1_h, w1f.at[0]), load(n1_h, w1f.at[1])]
    for s in range(1, 4):
        store_loads.append(load(store_h.at[block(graphs[s], rows)], store.at[s]))
    w2_loads = [load(s2_h, w2f.at[0]), load(n2_h, w2f.at[1])]
    up_load = load(up_h.at[member], upg.at[block(member, own)])

    packs = rows // 16
    middle = rows // 2
    spot = lax.broadcasted_iota(jnp.int32, (packs, 16, 128), 0) * 16
    spot = spot + lax.broadcasted_iota(jnp.int32, (packs, 16, 128), 1) - middle
    grid[...] = spot.astype(f32).astype(bf16)
    rec_t[...] = jnp.ones_like(rec_t)
    one_b, none_b = jnp.ones((), bf16), jnp.zeros((), bf16)
    slot = lax.broadcasted_iota(jnp.int32, (slots, 128), 0)
    group = 8

    def pieces(adj, hot, layer, graph):
        todo = []
        for c in range(rows // 128):
            lane = pl.ds(pl.multiple_of(graph * rows + c * 128, 128), 128)
            to = pl.ds(c * 128, 128)

            def prepare(lane=lane):
                used = slot < counts[layer : layer + 1, lane]
                ids = jnp.where(used, nbr[layer, :, lane], 4 * rows)
                ids = (ids - middle).astype(f32)
                keys = [
                    jnp.broadcast_to(ids[k : k + 1], (16, 128)).astype(bf16) for k in range(slots)
                ]
                if hot is None:
                    return keys
                at = (vertex[0:1, lane] - middle).astype(f32)
                return keys + [jnp.broadcast_to(at, (16, 128)).astype(bf16)]

            kept = []
            for j in range(packs // group):

                def unit(j=j, prepare=prepare, kept=kept, to=to):
                    if not kept:
                        kept.append(prepare())
                    keys = kept[0]
                    span = pl.ds(j * group, group)
                    lanes = grid[span]
                    total = jnp.where(keys[0][None] == lanes, one_b, none_b)
                    for k in range(1, slots):
                        total = total + jnp.where(keys[k][None] == lanes, one_b, none_b)
                    adj[span, :, to] = total
                    if hot is not None:
                        hot[span, :, to] = jnp.where(keys[slots][None] == lanes, one_b, none_b)

                todo.append(unit)
        return todo

    def square(ref):
        return ref[...].reshape(rows, rows)

    tn = ((0,), (0,))
    nt = ((1,), (1,))

    with jax.named_scope("barrier"):
        pl.semaphore_wait(barrier, 7)
    up_copies = [copy(up_h.at[p], upg.at[block(member, own)], node, p) for p in peers]
    for one in up_copies[1:] + up_copies[:1]:
        one.start()
    for one in id_loads:
        one.wait()
    with jax.named_scope("first_build"):
        for unit in pieces(adj_even, hot_even, 0, graphs[0]):
            unit()
        for s in range(4):
            rec_t[s : s + 1] = 1.0 / counts[0:1, block(graphs[s], rows)].astype(f32)
        rec_t[4:5] = 1.0 / counts[1:2, block(member, rows)].astype(f32)
        rec[...] = jnp.transpose(rec_t[...])

    for one in w1_loads:
        one.wait()
    wh[:cols], wl[:cols], wt[:cols] = thirds(w1f[0])
    wh[cols:], wl[cols:], wt[cols:] = thirds(w1f[1])

    side = rows // 2
    pin_copies = [
        copy(part.at[s, block(1 - cc, side)], pin.at[s], node, partner) for s in range(2)
    ]
    far_send, far_recv = take(2), 0
    far_recv = far_send
    far_copies = [
        copy(
            psum.at[s],
            far.at[block(cc, side)],
            node,
            (1 - yc) * 2 + s,
            send=far_send + s,
            recv=far_recv + cc,
        )
        for s in range(2)
    ]
    far_waits = [
        copy(
            psum.at[i],
            far.at[pl.ds(i * side, side)],
            node,
            across,
            send=far_send + i,
            recv=far_recv + i,
        )
        for i in range(2)
    ]
    near_copy = copy(part.at[2], near, node, partner)

    def pass_on(s):
        pin_copies[s].wait_recv()
        psum[s] = part[s, block(cc, side)] + pin[s]
        far_copies[s].start()

    tiles = rows // 128
    for s in range(4):
        adj, hot = (adj_even, hot_even) if s % 2 == 0 else (adj_odd, hot_odd)
        adj_next, hot_next = (adj_odd, hot_odd) if s % 2 == 0 else (adj_even, hot_even)
        with jax.named_scope(f"graph{s}"):
            store_loads[s].wait()
            if s < 3:
                todo = pieces(adj_next, hot_next, 0, graphs[s + 1])
            else:
                todo = pieces(adj_next, None, 1, member)
            per = -(-len(todo) // (2 * tiles))

            def some():
                for _ in range(per):
                    if todo:
                        todo.pop(0)()

            kept = jnp.concatenate(thirds(store[s]), axis=1)
            for t in range(tiles):
                span = pl.ds(t * 128, 128)
                pick = hot[:, :, span].reshape(rows, 128)
                found = mul(pick, kept, tn)
                xh[s, span, :cols] = found[:, :cols].astype(bf16)
                xl[s, span, :cols] = found[:, cols : 2 * cols].astype(bf16)
                xt[span, :cols] = found[:, 2 * cols :].astype(bf16)
                some()
            if s == 1 or s == 2:
                pass_on(s - 1)
            source = jnp.concatenate([xt[:, :cols], xl[s, :, :cols], xh[s, :, :cols]], axis=1)
            for t in range(tiles):
                span = pl.ds(t * 128, 128)
                pick = adj[:, :, span].reshape(rows, 128)
                agg = mul(pick, source, tn)
                agg = agg[:, :cols] + agg[:, cols : 2 * cols] + agg[:, 2 * cols :]
                ah, al, at = thirds(agg * rec[span, s : s + 1])
                xh[s, span, cols:] = ah
                xl[s, span, cols:] = al
                xt[span, cols:] = at
                part[s, span] = mul6(
                    (xh[s, span], xl[s, span], xt[span]), (wh[...], wl[...], wt[...])
                )
                some()
        if s < 2:
            pin_copies[s].start()
        if s == 2:
            near_copy.start()

    shrink = rec[:, 4:5]
    with jax.named_scope("back"):
        for one in w2_loads:
            one.wait()
        up_load.wait()
        for one in up_copies:
            one.wait_recv()
        scaled = halves(upg[...] * scale)
        w2s = halves(w2f[0])
        w2n = halves(w2f[1])
        back = halves(mul3(scaled, w2n, nt) * shrink)
        adj = square(adj_even)
        hg[...] = mul3(scaled, w2s, nt) + mul(adj, back[0]) + mul(adj, back[1])

    wing = width // 2
    pg_partner = copy(pg.at[3], pg.at[2], node, partner)
    halls = [(h, pl.ds(r * side, side)) for h in range(2) for r in range(2)]
    pg_across = [copy(pg.at[3, h, r], pg.at[cc, h, r], node, across) for h, r in halls]
    pg_forward = [copy(pg.at[cc, h, r], pg.at[cc, h, r], node, partner) for h, r in halls]
    with jax.named_scope("norm"):
        near_copy.wait_recv()
        for i in range(2):
            far_waits[i].wait_recv()
            span = pl.ds(i * side, side)
            pre = part[3, span] + near[span] + far[span]
            hidden, activated, inverse = normed_parts(pre)
            hid[span] = hidden
            gradient = norm_backward(hg[span], activated, inverse, pre)
            pg[3, 0, span] = gradient[:, :wing]
            pg[3, 1, span] = gradient[:, wing:]
            pg_across[i].start()
        pg_across[2].start()
        pg_across[3].start()
        pg_partner.start()

    with jax.named_scope("second_gradients"):
        hidden = halves(hid[...])
        adj = square(adj_even)
        agg_one = halves((mul(adj, hidden[0], tn) + mul(adj, hidden[1], tn)) * shrink)
        scaled = halves(upg[...] * scale)
        g2acc[0] = mul3(hidden, scaled, tn)
        g2acc[1] = mul3(agg_one, scaled, tn)
        g2_partner = copy(g2acc.at[1 - cc], g2p, node, partner)
        g2_partner.start()
    with jax.named_scope("output"):
        w2s = halves(w2f[0])
        w2n = halves(w2f[1])
        outg[...] = mul3(hidden, w2s) + mul3(agg_one, w2n)
    out_copies = [copy(outg.at[block(p, own)], out_ref.at[member], node, p) for p in peers]
    out_ref[member] = outg[block(member, own)]

    def reduction(full, base, size, result, to, bufs, direct):
        size = size // 2
        x_in, x_sum, z_in, m_in = bufs[:4]
        away = pl.ds(pl.multiple_of(base + (1 - xc) * size, size), size)
        home = pl.ds(pl.multiple_of(base + xc * size, size), size)
        mine = pl.ds(pl.multiple_of(to + xc * size, size), size)
        one = dict(
            full=full,
            home=home,
            mine=mine,
            result=result,
            bufs=bufs,
            x=copy(full.at[away], x_in, x_peer, member),
            z=copy(x_sum, z_in, z_pair, member),
            m=copy(x_sum, m_in, z_mate, member),
            o=copy(result.at[mine], result.at[mine], z_pair, member),
            e=copy(result.at[mine], result.at[mine], x_peer, member),
        )
        if direct:
            one["k"] = copy(result.at[mine], result.at[mine], z_cross, member)
        return one

    chunk = 128
    chunks = g1acc.shape[1] // chunk
    crossing = ()
    sets = []
    for h in range(2):
        for e in range(chunks):
            bufs = [b.at[h * chunks + e] for b in (xin, half, zin, mid)]
            direct = h * chunks + e in crossing
            at = e * chunk
            sets.append(reduction(g1acc.at[h], at, chunk, g1_ref.at[h], at, bufs, direct))
    quarter = width // 2
    pairs = []
    for i in range(2):
        bufs = [b.at[i] for b in (xin2, half2, zin2, mid2)]
        to = pl.multiple_of(yc * quarter, quarter)
        pairs.append(reduction(g2acc.at[cc], i * quarter, quarter, g2_ref.at[cc], to, bufs, False))
    y_copy = copy(mid2.at[1 - yc], yin2, node, across)
    ours, theirs = block(yc, quarter), block(1 - yc, quarter)
    g2_near = copy(g2_ref.at[cc, ours], g2_ref.at[cc, ours], node, partner)
    g2_far = copy(g2_ref.at[cc, ours], g2_ref.at[cc, ours], node, across)
    g2_onward = copy(g2_ref.at[cc, theirs], g2_ref.at[cc, theirs], node, partner)

    def stage_x(one):
        x_in, x_sum = one["bufs"][:2]
        one["x"].wait_recv()
        x_sum[...] = one["full"][one["home"]] + x_in[...]

        @pl.when(outer)
        def _():
            one["z"].start()

    def stage_z(one):
        @pl.when(inner)
        def _():
            x_sum, z_in = one["bufs"][1:3]
            one["z"].wait_recv()
            x_sum[...] = x_sum[...] + z_in[...]
            one["m"].start()

    def spread(one):
        for key in ("o", "k", "e"):
            if key in one:
                one[key].start()

    def stage_m(one):
        @pl.when(inner)
        def _():
            x_sum, z_in, m_in = one["bufs"][1:4]
            one["m"].wait_recv()
            if one is pairs[0] or one is pairs[1]:
                m_in[...] = x_sum[...] + m_in[...]
                if one is pairs[1]:
                    y_copy.start()
            else:
                one["result"][one["mine"]] = x_sum[...] + m_in[...]
                spread(one)

    def stage_y(one):
        @pl.when(inner)
        def _():
            y_copy.wait_recv()
            one["result"][one["mine"]] = mid2[yc] + yin2[...]
            spread(one)

    def stage_o(one):
        @pl.when(outer)
        def _():
            one["o"].wait_recv()
            if "k" not in one:
                one["e"].start()

    def stage_e(one):
        if "k" not in one:
            one["e"].wait_recv()
            return

        @pl.when(outer)
        def _():
            one["k"].wait_recv()

        @pl.when(inner)
        def _():
            one["e"].wait_recv()

    def g2_out(role):
        @pl.when(role)
        def _():
            pairs[0]["e"].wait_recv()
            g2_far.start()
            g2_near.start()

    def g2_on():
        g2_far.wait_recv()
        g2_onward.start()

    def both(k):
        return xh[k], xl[k]

    g2_partner.wait_recv()
    g2acc[cc] = g2acc[cc] + g2p[...]
    for one in pairs:
        one["x"].start()
    with jax.named_scope("early_gradients"):
        for h in range(2):
            g1acc[h] = mul3(both(3), halves(pg[3, h]), tn)
        pg_partner.wait_recv()
        for h in range(2):
            g1acc[h] += mul3(both(2), halves(pg[2, h]), tn)

    def arrive(h):
        with jax.named_scope(f"across_wait{h}"):
            for i in (2 * h, 2 * h + 1):
                pg_across[i].wait_recv()
                pg_forward[i].start()

    def late(h):
        with jax.named_scope(f"late_gradients{h}"):
            g1acc[h] += mul3(both(cc), halves(pg[cc, h]), tn)

    def forwarded(h):
        with jax.named_scope(f"forward_wait{h}"):
            for i in (2 * h, 2 * h + 1):
                pg_forward[i].wait_recv()

    def last(h, c):
        other = 1 - cc
        with jax.named_scope(f"last_gradients{h}{c}"):
            span = pl.ds(c * chunk, chunk)
            picked = (xh[other, :, span], xl[other, :, span])
            g1acc[h, span] += mul3(picked, halves(pg[other, h]), tn)
            sets[h * chunks + c]["x"].start()

    named = dict(X=stage_x, Z=stage_z, M=stage_m, O=stage_o, E=stage_e, Y=stage_y)

    def go(text):
        for word in text.split():
            with jax.named_scope(word):
                if word[1] == "g":
                    named[word[0]](pairs[int(word[2])])
                else:
                    named[word[0]](sets[int(word[1])])

    go("Xg0 Xg1")
    arrive(0)
    late(0)
    forwarded(0)
    for c in range(chunks):
        last(0, c)
    arrive(1)
    late(1)
    go("Zg0 Zg1")
    forwarded(1)
    for c in range(chunks):
        last(1, c)
    go("X0 X1 X2 X3 Mg0 Mg1")
    for one in out_copies[1:] + out_copies[:1]:
        one.start()
    go("X4 Z0 X5 Z1 X6 Z2 X7 Z3 Z4 Yg0 M0 Z5 M1 Z6 M2 Z7 M3 M4")
    g2_out(inner)
    go("M5 M6 M7")
    go("Og0 O0 O1 O2 O3 O4")
    g2_out(outer)
    go("O5 O6 O7 E0 E1 E2 E3 E4 E5 E6")
    with jax.named_scope("g2_on"):
        g2_on()
    go("E7")
    with jax.named_scope("g2_last"):
        g2_near.wait_recv()
        g2_onward.wait_recv()

    with jax.named_scope("drain"):
        for one in up_copies + pin_copies + [near_copy, pg_partner] + pg_across + pg_forward:
            one.wait_send()
        for one in far_copies + [g2_partner, g2_near, g2_far, g2_onward]:
            one.wait_send()
        for one in out_copies:
            one.wait()
        for one in sets + pairs:
            one["x"].wait_send()

        @pl.when(outer)
        def _():
            for one in sets + pairs:
                one["z"].wait_send()
            for one in sets + pairs[:1]:
                if "k" not in one:
                    one["e"].wait_send()

        @pl.when(inner)
        def _():
            for one in sets + pairs:
                one["m"].wait_send()
            for one in sets + pairs[:1]:
                for key in ("o", "k", "e"):
                    if key in one:
                        one[key].wait_send()
            y_copy.wait_send()


def place_kernel(out_ref, g1_ref, g2_ref, out, gs1, gn1, gs2, gn2, sems):
    cols, wing = gs1.shape[0], g1_ref.shape[2]
    pairs = [(out_ref, out), (g2_ref.at[0], gs2), (g2_ref.at[1], gn2)]
    for h in range(2):
        span = pl.ds(h * wing, wing)
        pairs.append((g1_ref.at[h, pl.ds(0, cols)], gs1.at[:, span]))
        pairs.append((g1_ref.at[h, pl.ds(cols, cols)], gn1.at[:, span]))
    copies = [pltpu.make_async_copy(a, b, sems.at[i]) for i, (a, b) in enumerate(pairs)]
    for one in copies:
        one.start()
    for one in copies:
        one.wait()


def fused(mesh_node):
    def run(stored, vertex, neighbors, counts, self_w1, neigh_w1, self_w2, neigh_w2, upstream):
        graphs, own, width = upstream.shape
        rows = vertex.shape[0] // graphs
        slots = neighbors.shape[2]
        cols = stored.shape[1]
        total = vertex.shape[0]
        turned = jnp.transpose(neighbors, (0, 2, 1))
        scale = 1.0 / math.sqrt(total * mesh_node)
        wide = 2 * cols
        wing = width // 2
        chunks = 2 * (wide // 128)
        vm = pltpu.VMEM
        scratch = [
            vm((4, rows, cols), f32),
            vm(turned.shape, jnp.int32),
            vm((1, total), jnp.int32),
            vm(counts.shape, jnp.int32),
            vm((2, cols, width), f32),
            vm((2, width, width), f32),
            vm((rows, width), f32),
            vm((rows // 16, 16, 128), bf16),
            vm((rows // 16, 16, rows), bf16),
            vm((rows // 16, 16, rows), bf16),
            vm((rows // 16, 16, rows), bf16),
            vm((rows // 16, 16, rows), bf16),
            vm((128, rows), f32),
            vm((rows, 128), f32),
            vm((4, rows, width), f32),
            vm((2, rows // 2, width), f32),
            vm((2, rows // 2, width), f32),
            vm((rows, width), f32),
            vm((rows, width), f32),
            vm((4, 2, rows, wing), f32),
            vm((4, rows, wide), bf16),
            vm((4, rows, wide), bf16),
            vm((rows, wide), bf16),
            vm((wide, width), bf16),
            vm((wide, width), bf16),
            vm((wide, width), bf16),
            vm((rows, width), f32),
            vm((rows, width), f32),
            vm((2, wide, wing), f32),
            vm((2, width, width), f32),
            vm((width, width), f32),
            vm((rows, width), f32),
        ]
        scratch += [vm((chunks, 64, wing), f32) for _ in range(4)]
        scratch += [vm((2, width // 4, width), f32) for _ in range(4)]
        scratch += [vm((width // 4, width), f32)]
        scratch += [
            pltpu.SemaphoreType.DMA((16,)),
            pltpu.SemaphoreType.DMA((48 + 5 * chunks,)),
            pltpu.SemaphoreType.DMA((48 + 5 * chunks,)),
        ]
        anywhere = pl.BlockSpec(memory_space=pl.ANY)
        fast = pl.BlockSpec(memory_space=pltpu.VMEM)
        held = pl.pallas_call(
            functools.partial(fused_kernel, slots, scale),
            out_shape=(
                pltpu.VMEM((graphs, own, width), f32),
                pltpu.VMEM((2, wide, wing), f32),
                pltpu.VMEM((2, width, width), f32),
            ),
            in_specs=[anywhere] * 9,
            out_specs=(fast,) * 3,
            scratch_shapes=scratch,
            compiler_params=pltpu.CompilerParams(
                collective_id=0, has_side_effects=True, vmem_limit_bytes=60 * 1024 * 1024
            ),
        )(stored, turned, vertex[None], counts, self_w1, neigh_w1, self_w2, neigh_w2, upstream)
        first = jax.ShapeDtypeStruct((cols, width), f32)
        later = jax.ShapeDtypeStruct((width, width), f32)
        return pl.pallas_call(
            place_kernel,
            out_shape=(jax.ShapeDtypeStruct((graphs, own, width), f32), first, first, later, later),
            in_specs=[anywhere] * 3,
            out_specs=(anywhere,) * 5,
            scratch_shapes=[pltpu.SemaphoreType.DMA((7,))],
        )(*[pltpu.with_memory_space_constraint(one, pltpu.VMEM) for one in held])

    return run


def fitted(mesh):
    node_total, members = mesh.shape["node"], mesh.shape["mp"]

    def run(*args):
        vertex, upstream, stored = args[1], args[8], args[0]
        graphs, own, width = upstream.shape
        fits = (
            members == 4
            and graphs == members
            and node_total == 8
            and own == 128
            and own * members * graphs == vertex.shape[0]
            and args[2].shape[2] % 8 == 0
            and width == 256
            and stored.shape[1] == width
        )
        return (fused(node_total) if fits else body)(*args)

    return run


def solution(mesh):
    placed = (
        P("node", "mp"),
        P("node"),
        P(None, "node", None),
        P(None, "node"),
        P("mp", None),
        P("mp", None),
        P(),
        P(),
        P("node", "mp", None),
    )
    return jax.shard_map(
        fitted(mesh),
        mesh=mesh,
        in_specs=placed,
        out_specs=(P("node", "mp", None), P("mp", None), P("mp", None), P(), P()),
        check_vma=False,
    )
```

```python
import functools
import math

import jax
import jax.numpy as jnp
from jax import lax
from jax.experimental import pallas as pl
from jax.experimental.pallas import tpu as pltpu
from jax.sharding import PartitionSpec as P

epsilon = 1e-05
precise = lax.Precision.HIGHEST


def adjacency(neighbor_ids, row_counts, width):
    row_total = neighbor_ids.shape[0]
    slot_positions = neighbor_ids.shape[1]
    tile_rows = min(128, row_total)
    tiles = row_total // tile_rows
    column_ids = jnp.arange(width, dtype=jnp.int32)
    slot_ids = jnp.arange(slot_positions, dtype=jnp.int32)
    slot_weight = (slot_ids[None, :] < row_counts[:, None]).astype(jnp.float32) / row_counts[
        :, None
    ].astype(jnp.float32)

    def one_tile(packed):
        tile_ids, tile_weight = packed
        hits = (tile_ids[:, :, None] == column_ids[None, None, :]).astype(jnp.float32)
        return jnp.sum(hits * tile_weight[:, :, None], axis=1)

    tiled = lax.map(
        one_tile,
        (
            neighbor_ids.reshape(tiles, tile_rows, slot_positions),
            slot_weight.reshape(tiles, tile_rows, slot_positions),
        ),
    )
    return tiled.reshape(row_total, width)


def normed_parts(pre_act):
    activated = jnp.maximum(pre_act, 0.0)
    inverse = lax.rsqrt(jnp.mean(activated * activated, axis=1, keepdims=True) + epsilon)
    return (activated * inverse, activated, inverse)


def norm_backward(hidden_grad, activated, inverse, pre_act):
    inner_sum = jnp.mean(hidden_grad * activated, axis=1, keepdims=True)
    act_grad = inverse * hidden_grad - activated * (inverse * inverse * inverse) * inner_sum
    return jnp.where(pre_act > 0, act_grad, 0.0)


def body(
    stored_features,
    vertex_row_index,
    neighbors,
    counts,
    self_w1,
    neigh_w1,
    self_w2,
    neigh_w2,
    upstream,
):
    mp_index = lax.axis_index("mp")
    sampled_graphs = upstream.shape[0]
    own_rows = upstream.shape[1]
    row_grand_total = vertex_row_index.shape[0] // sampled_graphs
    column_total = stored_features.shape[1]
    slot_positions = neighbors.shape[2]
    gradient_scale = 1.0 / math.sqrt(row_grand_total * sampled_graphs * lax.axis_size("node"))
    first_row = mp_index * own_rows
    stored_blocks = stored_features.reshape(sampled_graphs, row_grand_total, column_total)
    vertex_blocks = vertex_row_index.reshape(sampled_graphs, row_grand_total)
    neighbor_blocks = jnp.transpose(
        neighbors.reshape(2, sampled_graphs, row_grand_total, slot_positions), (1, 0, 2, 3)
    )
    block_count = jnp.transpose(counts.reshape(2, sampled_graphs, row_grand_total), (1, 0, 2))

    def one_graph(carry, packed):
        store_rows, node_rows, neighbor_ids, row_counts, cotangent = packed
        features = jnp.take(store_rows, node_rows, axis=0)
        adj_zero = adjacency(neighbor_ids[0], row_counts[0], row_grand_total)
        agg_zero = jnp.dot(adj_zero, features, precision=precise)
        own_ids = lax.dynamic_slice_in_dim(neighbor_ids[1], first_row, own_rows, 0)
        own_counts = lax.dynamic_slice_in_dim(row_counts[1], first_row, own_rows, 0)
        adj_own = adjacency(own_ids, own_counts, row_grand_total)
        scaled = cotangent * gradient_scale
        back_neigh = jnp.dot(scaled, neigh_w2.T, precision=precise)
        back_self = jnp.dot(scaled, self_w2.T, precision=precise)
        contrib = lax.dot_general(adj_own, back_neigh, (((0,), (0,)), ((), ())), precision=precise)
        rows_self = features
        rows_neigh = agg_zero
        pre_own = lax.psum_scatter(
            jnp.dot(rows_self, self_w1, precision=precise)
            + jnp.dot(rows_neigh, neigh_w1, precision=precise),
            "mp",
            scatter_dimension=0,
            tiled=True,
        )
        hidden_own, act_own, inverse_own = normed_parts(pre_own)
        hidden_all = lax.all_gather(hidden_own, "mp", axis=0, tiled=True)
        agg_one = jnp.dot(adj_own, hidden_all, precision=precise)
        hidden_grad = lax.psum_scatter(contrib, "mp", scatter_dimension=0, tiled=True) + back_self
        pre_grad = norm_backward(hidden_grad, act_own, inverse_own, pre_own)
        grad_piece = lax.all_gather(pre_grad, "mp", axis=0, tiled=True)
        rows_self = features
        rows_neigh = agg_zero
        step_self1 = carry[0] + jnp.dot(rows_self.T, grad_piece, precision=precise)
        step_neigh1 = carry[1] + jnp.dot(rows_neigh.T, grad_piece, precision=precise)
        graph_out = jnp.dot(hidden_own, self_w2, precision=precise) + jnp.dot(
            agg_one, neigh_w2, precision=precise
        )
        step_self2 = carry[2] + jnp.dot(hidden_own.T, scaled, precision=precise)
        step_neigh2 = carry[3] + jnp.dot(agg_one.T, scaled, precision=precise)
        return ((step_self1, step_neigh1, step_self2, step_neigh2), graph_out)

    zero_first = jnp.zeros(self_w1.shape, jnp.float32)
    zero_second = jnp.zeros(self_w2.shape, jnp.float32)
    totals, layer_out = lax.scan(
        one_graph,
        (zero_first, zero_first, zero_second, zero_second),
        (stored_blocks, vertex_blocks, neighbor_blocks, block_count, upstream),
    )
    grad_self1, grad_neigh1, grad_self2, grad_neigh2 = totals
    grad_self1, grad_neigh1, grad_self2, grad_neigh2 = lax.psum(
        (grad_self1, grad_neigh1, grad_self2, grad_neigh2), "node"
    )
    grad_self2, grad_neigh2 = lax.psum((grad_self2, grad_neigh2), "mp")
    return (layer_out, grad_self1, grad_neigh1, grad_self2, grad_neigh2)


f32 = jnp.float32
bf16 = jnp.bfloat16


def halves(value):
    high = value.astype(bf16)
    return high, (value - high.astype(f32)).astype(bf16)


def thirds(value):
    high = value.astype(bf16)
    rest = value - high.astype(f32)
    middle = rest.astype(bf16)
    return high, middle, (rest - middle.astype(f32)).astype(bf16)


def mul(left, right, dims=((1,), (0,))):
    return lax.dot_general(left, right, (dims, ((), ())), preferred_element_type=f32)


def mul3(left, right, dims=((1,), (0,))):
    return (
        mul(left[0], right[0], dims) + mul(left[1], right[0], dims) + mul(left[0], right[1], dims)
    )


def mul6(left, right):
    small = mul(left[2], right[0]) + mul(left[0], right[2]) + mul(left[1], right[1])
    return mul(left[0], right[0]) + (mul(left[0], right[1]) + mul(left[1], right[0]) + small)


def fused_kernel(
    slots,
    scale,
    store_h,
    nbr_h,
    vertex_h,
    counts_h,
    s1_h,
    n1_h,
    s2_h,
    n2_h,
    up_h,
    out_ref,
    g1_ref,
    g2_ref,
    store,
    nbr,
    vertex,
    counts,
    w1f,
    w2f,
    upg,
    grid,
    adj_even,
    adj_odd,
    hot_even,
    hot_odd,
    rec_t,
    rec,
    part,
    pin,
    psum,
    near,
    far,
    pg,
    xh,
    xl,
    xt,
    wh,
    wl,
    wt,
    hid,
    hg,
    g1acc,
    g2acc,
    g2p,
    outg,
    xin,
    half,
    zin,
    mid,
    xin2,
    half2,
    zin2,
    mid2,
    yin2,
    load_sems,
    send_sems,
    recv_sems,
):
    rows, width = upg.shape
    own = up_h.shape[1]
    cols = store_h.shape[1]
    node = lax.axis_index("node")
    member = lax.axis_index("mp")
    zc, xc = node // 2, node % 2
    yc, cc = member // 2, member % 2
    partner = yc * 2 + (1 - cc)
    across = (1 - yc) * 2 + cc
    diagonal = (1 - yc) * 2 + (1 - cc)
    peers = (partner, across, diagonal)
    x_peer = zc * 2 + (1 - xc)
    z_pair = (zc + 1 - 2 * (zc % 2)) * 2 + xc
    z_mate = (3 - zc) * 2 + xc
    inner = jnp.logical_or(zc == 1, zc == 2)
    outer = jnp.logical_or(zc == 0, zc == 3)
    graphs = ((1 - yc) * 2, (1 - yc) * 2 + 1, partner, member)

    def target(node_id, member_id):
        return dict(device_id=(node_id, member_id), device_id_type=pl.DeviceIdType.MESH)

    sending, receiving = {}, {}

    def place(table, key):
        key = ("own", len(table)) if key is None else key
        return table.setdefault(key, len(table))

    def copy(source, dest, node_id, member_id, send=None, recv=None, slot=None):
        return pltpu.make_async_remote_copy(
            src_ref=source,
            dst_ref=dest,
            send_sem=send_sems.at[place(sending, send)],
            recv_sem=recv_sems.at[place(receiving, recv) if slot is None else slot],
            **target(node_id, member_id),
        )

    def sent(key, ref):
        copy(ref, ref, node, partner, send=key, recv="out").wait_send()

    def received(key, ref):
        copy(ref, ref, node, partner, send="out", recv=key).wait_recv()

    def block(index, size):
        return pl.ds(pl.multiple_of(index * size, size), size)

    loading = {}

    def local(source, dest, key=None):
        return pltpu.make_async_copy(source, dest, load_sems.at[place(loading, key)])

    def load(source, dest, key=None):
        one = local(source, dest, key)
        one.start()
        return one

    barrier = pltpu.get_barrier_semaphore()
    for p in peers:
        pl.semaphore_signal(barrier, inc=1, **target(node, p))
    pl.semaphore_signal(barrier, inc=1, **target(x_peer, member))
    pl.semaphore_signal(barrier, inc=1, **target(z_pair, member))
    pl.semaphore_signal(barrier, inc=1, **target(z_mate, member))

    id_loads = [load(nbr_h, nbr), load(vertex_h, vertex), load(counts_h, counts)]
    store_loads = [load(store_h.at[block(graphs[0], rows)], store.at[0])]
    load(s1_h, w1f.at[0], "w1")
    load(n1_h, w1f.at[1], "w1")
    for s in range(1, 4):
        store_loads.append(load(store_h.at[block(graphs[s], rows)], store.at[s]))
    load(s2_h, w2f.at[0], "w2")
    load(n2_h, w2f.at[1], "w2")
    up_load = load(up_h.at[member], upg.at[block(member, own)])

    packs = rows // 16
    middle = rows // 2
    spot = lax.broadcasted_iota(jnp.int32, (packs, 16, 128), 0) * 16
    spot = spot + lax.broadcasted_iota(jnp.int32, (packs, 16, 128), 1) - middle
    grid[...] = spot.astype(f32).astype(bf16)
    rec_t[...] = jnp.ones_like(rec_t)
    one_b, none_b = jnp.ones((), bf16), jnp.zeros((), bf16)
    slot = lax.broadcasted_iota(jnp.int32, (slots, 128), 0)
    group = 8

    def pieces(adj, hot, layer, graph):
        todo = []
        for c in range(rows // 128):
            lane = pl.ds(pl.multiple_of(graph * rows + c * 128, 128), 128)
            to = pl.ds(c * 128, 128)

            def prepare(lane=lane):
                used = slot < counts[layer : layer + 1, lane]
                ids = jnp.where(used, nbr[layer, :, lane], 4 * rows)
                ids = (ids - middle).astype(f32)
                keys = [
                    jnp.broadcast_to(ids[k : k + 1], (16, 128)).astype(bf16) for k in range(slots)
                ]
                if hot is None:
                    return keys
                at = (vertex[0:1, lane] - middle).astype(f32)
                return keys + [jnp.broadcast_to(at, (16, 128)).astype(bf16)]

            kept = []
            for j in range(packs // group):

                def unit(j=j, prepare=prepare, kept=kept, to=to):
                    if not kept:
                        kept.append(prepare())
                    keys = kept[0]
                    span = pl.ds(j * group, group)
                    lanes = grid[span]
                    total = jnp.where(keys[0][None] == lanes, one_b, none_b)
                    for k in range(1, slots):
                        total = total + jnp.where(keys[k][None] == lanes, one_b, none_b)
                    adj[span, :, to] = total
                    if hot is not None:
                        hot[span, :, to] = jnp.where(keys[slots][None] == lanes, one_b, none_b)

                todo.append(unit)
        return todo

    def square(ref):
        return ref[...].reshape(rows, rows)

    tn = ((0,), (0,))
    nt = ((1,), (1,))

    with jax.named_scope("barrier"):
        pl.semaphore_wait(barrier, 6)
    up_copies = [
        copy(up_h.at[p], upg.at[block(member, own)], node, p, send="up", recv="up") for p in peers
    ]
    three = pl.ds(0, 3 * own)
    for one in up_copies[1:] + up_copies[:1]:
        one.start()
    for one in id_loads:
        one.wait()
    with jax.named_scope("first_build"):
        for unit in pieces(adj_even, hot_even, 0, graphs[0]):
            unit()
        for s in range(4):
            rec_t[s : s + 1] = 1.0 / counts[0:1, block(graphs[s], rows)].astype(f32)
        rec_t[4:5] = 1.0 / counts[1:2, block(member, rows)].astype(f32)
        rec[...] = jnp.transpose(rec_t[...])

    local(w1f, w1f, "w1").wait()
    wh[:cols], wl[:cols], wt[:cols] = thirds(w1f[0])
    wh[cols:], wl[cols:], wt[cols:] = thirds(w1f[1])

    side = rows // 2
    pin_copies = [
        copy(part.at[s, block(1 - cc, side)], pin.at[s], node, partner, send="pin")
        for s in range(2)
    ]
    far_slot = place(receiving, "far0")
    place(receiving, "far1")
    far_copies = [
        copy(
            psum.at[s],
            far.at[block(cc, side)],
            node,
            (1 - yc) * 2 + s,
            send="far",
            slot=far_slot + cc,
        )
        for s in range(2)
    ]
    far_waits = [
        copy(
            psum.at[i],
            far.at[pl.ds(i * side, side)],
            node,
            across,
            send="far",
            recv=f"far{i}",
        )
        for i in range(2)
    ]
    near_copy = copy(part.at[2], near, node, partner)

    def pass_on(s):
        pin_copies[s].wait_recv()
        psum[s] = part[s, block(cc, side)] + pin[s]
        far_copies[s].start()

    tiles = rows // 128
    for s in range(4):
        adj, hot = (adj_even, hot_even) if s % 2 == 0 else (adj_odd, hot_odd)
        adj_next, hot_next = (adj_odd, hot_odd) if s % 2 == 0 else (adj_even, hot_even)
        with jax.named_scope(f"graph{s}"):
            store_loads[s].wait()
            if s < 3:
                todo = pieces(adj_next, hot_next, 0, graphs[s + 1])
            else:
                todo = pieces(adj_next, None, 1, member)
            per = -(-len(todo) // (2 * tiles))

            def some():
                for _ in range(per):
                    if todo:
                        todo.pop(0)()

            kept = jnp.concatenate(thirds(store[s]), axis=1)
            for t in range(tiles):
                span = pl.ds(t * 128, 128)
                pick = hot[:, :, span].reshape(rows, 128)
                found = mul(pick, kept, tn)
                xh[s, span, :cols] = found[:, :cols].astype(bf16)
                xl[s, span, :cols] = found[:, cols : 2 * cols].astype(bf16)
                xt[span, :cols] = found[:, 2 * cols :].astype(bf16)
                some()
                if t == 2 and (s == 1 or s == 2):
                    pass_on(s - 1)
            source = jnp.concatenate([xt[:, :cols], xl[s, :, :cols], xh[s, :, :cols]], axis=1)
            for t in range(tiles):
                span = pl.ds(t * 128, 128)
                pick = adj[:, :, span].reshape(rows, 128)
                agg = mul(pick, source, tn)
                agg = agg[:, :cols] + agg[:, cols : 2 * cols] + agg[:, 2 * cols :]
                ah, al, at = thirds(agg * rec[span, s : s + 1])
                xh[s, span, cols:] = ah
                xl[s, span, cols:] = al
                xt[span, cols:] = at
                part[s, span] = mul6(
                    (xh[s, span], xl[s, span], xt[span]), (wh[...], wl[...], wt[...])
                )
                some()
        if s < 2:
            pin_copies[s].start()
        if s == 2:
            near_copy.start()

    shrink = rec[:, 4:5]
    with jax.named_scope("back"):
        local(w2f, w2f, "w2").wait()
        up_load.wait()
        received("up", upg.at[three])
        scaled = halves(upg[...] * scale)
        w2s = halves(w2f[0])
        w2n = halves(w2f[1])
        back = halves(mul3(scaled, w2n, nt) * shrink)
        adj = square(adj_even)
        hg[...] = mul3(scaled, w2s, nt) + mul(adj, back[0]) + mul(adj, back[1])

    wing = width // 2
    pg_partner = copy(pg.at[3], pg.at[2], node, partner)
    halls = [(h, pl.ds(r * side, side)) for h in range(2) for r in range(2)]
    pg_across = [copy(pg.at[3, h, r], pg.at[cc, h, r], node, across, send="pg") for h, r in halls]
    pg_forward = [
        copy(pg.at[cc, h, r], pg.at[cc, h, r], node, partner, send="onward", recv=("onward", h))
        for h, r in halls
    ]
    with jax.named_scope("norm"):
        near_copy.wait_recv()
        for i in range(2):
            far_waits[i].wait_recv()
            span = pl.ds(i * side, side)
            pre = part[3, span] + near[span] + far[span]
            hidden, activated, inverse = normed_parts(pre)
            hid[span] = hidden
            gradient = norm_backward(hg[span], activated, inverse, pre)
            pg[3, 0, span] = gradient[:, :wing]
            pg[3, 1, span] = gradient[:, wing:]
            pg_across[i].start()
        pg_across[2].start()
        pg_across[3].start()
        pg_partner.start()

    with jax.named_scope("second_gradients"):
        hidden = halves(hid[...])
        adj = square(adj_even)
        agg_one = halves((mul(adj, hidden[0], tn) + mul(adj, hidden[1], tn)) * shrink)
        scaled = halves(upg[...] * scale)
        g2acc[0] = mul3(hidden, scaled, tn)
        g2acc[1] = mul3(agg_one, scaled, tn)
        g2_partner = copy(g2acc.at[1 - cc], g2p, node, partner)
        g2_partner.start()
    with jax.named_scope("output"):
        w2s = halves(w2f[0])
        w2n = halves(w2f[1])
        outg[...] = mul3(hidden, w2s) + mul3(agg_one, w2n)
    out_copies = [
        copy(outg.at[block(p, own)], out_ref.at[member], node, p, send="out", recv="out")
        for p in peers
    ]
    out_here = load(outg.at[block(member, own)], out_ref.at[member])

    def reduction(full, base, size, result, to, bufs, held, tag):
        size = size // 2
        x_in, x_sum, z_in, m_in = bufs[:4]
        away = pl.ds(pl.multiple_of(base + (1 - xc) * size, size), size)
        home = pl.ds(pl.multiple_of(base + xc * size, size), size)
        mine = pl.ds(pl.multiple_of(to + xc * size, size), size)
        name, i = tag
        one = dict(
            full=full,
            home=home,
            mine=mine,
            result=result,
            bufs=bufs,
            x=copy(full.at[away], x_in, x_peer, member, send=(name, "x")),
            z=copy(x_sum, z_in, z_pair, member, send=(name, "z"), recv=(name, "z", i)),
            m=copy(x_sum, m_in, z_mate, member, send=(name, "z")),
            o=copy(held, result.at[mine], z_pair, member, send=(name, "o"), recv=(name, "z", i)),
            keep=local(held, result.at[mine], name),
        )
        for key, source in (("e", held), ("relay", result.at[mine])):
            one[key] = copy(
                source, result.at[mine], x_peer, member, send=(name, "e"), recv=(name, "e")
            )
        return one

    chunk = 128
    chunks = g1acc.shape[1] // chunk
    sets = []
    for h in range(2):
        for e in range(chunks):
            bufs = [b.at[h * chunks + e] for b in (xin, half, zin, mid)]
            at = e * chunk
            tag = (1, h * chunks + e)
            sets.append(
                reduction(g1acc.at[h], at, chunk, g1_ref.at[h], at, bufs, bufs[3], tag)
            )
    quarter = width // 2
    pairs = []
    for i in range(2):
        bufs = [b.at[i] for b in (xin2, half2, zin2, mid2)]
        to = pl.multiple_of(yc * quarter, quarter)
        pairs.append(
            reduction(
                g2acc.at[cc], i * quarter, quarter, g2_ref.at[cc], to, bufs, yin2, (2, i)
            )
        )
    y_copy = copy(mid2.at[1 - yc], yin2, node, across)
    ours = block(yc, quarter)
    slab = quarter // 2
    corner = [
        pl.ds(pl.multiple_of(a * quarter + b * slab, slab), slab)
        for a, b in ((yc, xc), (yc, 1 - xc), (1 - yc, xc), (1 - yc, 1 - xc))
    ]
    def g2_copy(source, r, member_id, recv):
        return copy(source, g2_ref.at[cc, r], node, member_id, send="g2", recv=recv)

    g2_near = g2_copy(g2_ref.at[cc, ours], ours, partner, "near")
    g2_far = [g2_copy(g2_ref.at[cc, corner[i]], corner[i], across, ("g2", i)) for i in range(2)]
    g2_first = g2_copy(yin2, corner[0], across, ("g2", 0))
    g2_onward = [g2_copy(g2_ref.at[cc, r], r, partner, "near") for r in corner[2:]]

    def stage_x(one):
        x_in, x_sum = one["bufs"][:2]
        one["x"].wait_recv()
        x_sum[...] = one["full"][one["home"]] + x_in[...]

        @pl.when(outer)
        def _():
            one["z"].start()

    def stage_z(one):
        @pl.when(inner)
        def _():
            x_sum, z_in = one["bufs"][1:3]
            one["z"].wait_recv()
            x_sum[...] = x_sum[...] + z_in[...]
            one["m"].start()

    def spread(one, held):
        one["o"].start()
        one["e"].start()
        one["keep"].start()

    def stage_m(one):
        @pl.when(inner)
        def _():
            x_sum, z_in, m_in = one["bufs"][1:4]
            one["m"].wait_recv()
            m_in[...] = x_sum[...] + m_in[...]
            if one is pairs[1]:
                y_copy.start()
            elif one is not pairs[0]:
                spread(one, m_in)

    def stage_y(one):
        @pl.when(inner)
        def _():
            y_copy.wait_recv()
            yin2[...] = mid2[yc] + yin2[...]
            spread(one, yin2)
            g2_first.start()

    def stage_o(one):
        @pl.when(outer)
        def _():
            one["o"].wait_recv()
            one["relay"].start()
            if one is pairs[0]:
                g2_far[0].start()

    def stage_e(one):
        one["e"].wait_recv()

    def g2_out(role):
        @pl.when(role)
        def _():
            pairs[0]["e"].wait_recv()
            if role is inner:
                pairs[0]["keep"].wait()
            g2_far[1].start()
            g2_near.start()

    def g2_on(i):
        with jax.named_scope(f"g2_on{i}"):
            g2_far[i].wait_recv()
            g2_onward[i].start()

    def both(k):
        return xh[k], xl[k]

    g2_partner.wait_recv()
    g2acc[cc] = g2acc[cc] + g2p[...]
    for one in pairs:
        one["x"].start()
    with jax.named_scope("early_gradients"):
        for h in range(2):
            g1acc[h] = mul3(both(3), halves(pg[3, h]), tn)
        pg_partner.wait_recv()
        for h in range(2):
            g1acc[h] += mul3(both(2), halves(pg[2, h]), tn)

    def arrive(h):
        with jax.named_scope(f"across_wait{h}"):
            for i in (2 * h, 2 * h + 1):
                pg_across[i].wait_recv()
                pg_forward[i].start()

    def late(h):
        with jax.named_scope(f"late_gradients{h}"):
            g1acc[h] += mul3(both(cc), halves(pg[cc, h]), tn)

    def forwarded(h):
        with jax.named_scope(f"forward_wait{h}"):
            received(("onward", h), pg.at[1 - cc, h])

    def last(h, c):
        other = 1 - cc
        with jax.named_scope(f"last_gradients{h}{c}"):
            span = pl.ds(c * chunk, chunk)
            picked = (xh[other, :, span], xl[other, :, span])
            g1acc[h, span] += mul3(picked, halves(pg[other, h]), tn)
            sets[h * chunks + c]["x"].start()

    named = dict(X=stage_x, Z=stage_z, M=stage_m, O=stage_o, E=stage_e, Y=stage_y)

    def go(*words):
        for word in words:
            with jax.named_scope(word):
                if word[1] == "g":
                    named[word[0]](pairs[int(word[2])])
                else:
                    named[word[0]](sets[int(word[1])])

    go("Xg0", "Xg1")
    arrive(0)
    late(0)
    forwarded(0)
    for c in range(chunks):
        last(0, c)
    go("Zg0", "Zg1")
    arrive(1)
    late(1)
    forwarded(1)
    for c in range(chunks):
        last(1, c)
    go("X0", "X1", "X2", "X3", "Mg0", "Mg1")
    for one in out_copies[1:] + out_copies[:1]:
        one.start()
    go("X4", "Z0", "X5", "Z1", "X6", "Z2", "X7", "Z3", "Z4", "Yg0", "M0", "Z5", "M1", "Z6", "M2", "Z7", "M3", "M4")
    g2_out(inner)
    go("M5", "M6", "M7")
    go("Og0", "O0", "O1", "O2", "O3", "O4")
    g2_out(outer)
    go("O5", "O6", "O7")
    g2_on(0)
    g2_on(1)
    with jax.named_scope("ends"):
        received((1, "e"), mid)
    with jax.named_scope("g2_last"):
        received("near", g2acc.at[0])

    with jax.named_scope("drain"):
        sent("up", upg.at[three])
        sent("pin", psum)
        sent("far", psum)
        near_copy.wait_send()
        pg_partner.wait_send()
        sent("pg", pg.at[3])
        sent("onward", pg.at[0])
        g2_partner.wait_send()
        sent("out", outg.at[three])
        received("out", outg.at[three])
        out_here.wait()
        sent("g2", outg.at[three])
        sent((1, "x"), xin)
        sent((1, "z"), zin)
        sent((1, "e"), mid)
        sent((2, "x"), xin2)
        sent((2, "z"), zin2)
        sent((2, "e"), yin2)

        @pl.when(inner)
        def _():
            sent((1, "o"), mid)
            sent((2, "o"), yin2)
            local(mid, mid, 1).wait()
            y_copy.wait_send()


def place_kernel(out_ref, g1_ref, g2_ref, out, gs1, gn1, gs2, gn2, sems):
    cols, wing = gs1.shape[0], g1_ref.shape[2]
    pairs = [(out_ref, out), (g2_ref.at[0], gs2), (g2_ref.at[1], gn2)]
    for h in range(2):
        span = pl.ds(h * wing, wing)
        pairs.append((g1_ref.at[h, pl.ds(0, cols)], gs1.at[:, span]))
        pairs.append((g1_ref.at[h, pl.ds(cols, cols)], gn1.at[:, span]))
    copies = [pltpu.make_async_copy(a, b, sems.at[i]) for i, (a, b) in enumerate(pairs)]
    for one in copies:
        one.start()
    for one in copies:
        one.wait()


def fused(mesh_node):
    def run(stored, vertex, neighbors, counts, self_w1, neigh_w1, self_w2, neigh_w2, upstream):
        graphs, own, width = upstream.shape
        rows = vertex.shape[0] // graphs
        slots = neighbors.shape[2]
        cols = stored.shape[1]
        total = vertex.shape[0]
        turned = jnp.transpose(neighbors, (0, 2, 1))
        scale = 1.0 / math.sqrt(total * mesh_node)
        wide = 2 * cols
        wing = width // 2
        chunks = 2 * (wide // 128)
        vm = pltpu.VMEM
        scratch = [
            vm((4, rows, cols), f32),
            vm(turned.shape, jnp.int32),
            vm((1, total), jnp.int32),
            vm(counts.shape, jnp.int32),
            vm((2, cols, width), f32),
            vm((2, width, width), f32),
            vm((rows, width), f32),
            vm((rows // 16, 16, 128), bf16),
            vm((rows // 16, 16, rows), bf16),
            vm((rows // 16, 16, rows), bf16),
            vm((rows // 16, 16, rows), bf16),
            vm((rows // 16, 16, rows), bf16),
            vm((128, rows), f32),
            vm((rows, 128), f32),
            vm((4, rows, width), f32),
            vm((2, rows // 2, width), f32),
            vm((2, rows // 2, width), f32),
            vm((rows, width), f32),
            vm((rows, width), f32),
            vm((4, 2, rows, wing), f32),
            vm((4, rows, wide), bf16),
            vm((4, rows, wide), bf16),
            vm((rows, wide), bf16),
            vm((wide, width), bf16),
            vm((wide, width), bf16),
            vm((wide, width), bf16),
            vm((rows, width), f32),
            vm((rows, width), f32),
            vm((2, wide, wing), f32),
            vm((2, width, width), f32),
            vm((width, width), f32),
            vm((rows, width), f32),
        ]
        scratch += [vm((chunks, 64, wing), f32) for _ in range(4)]
        scratch += [vm((2, width // 4, width), f32) for _ in range(4)]
        scratch += [vm((width // 4, width), f32)]
        scratch += [
            pltpu.SemaphoreType.DMA((13,)),
            pltpu.SemaphoreType.DMA((19,)),
            pltpu.SemaphoreType.DMA((51,)),
        ]
        anywhere = pl.BlockSpec(memory_space=pl.ANY)
        held = pl.pallas_call(
            functools.partial(fused_kernel, slots, scale),
            out_shape=(
                pltpu.VMEM((graphs, own, width), f32),
                pltpu.VMEM((2, wide, wing), f32),
                pltpu.VMEM((2, width, width), f32),
            ),
            in_specs=[anywhere] * 9,
            out_specs=(anywhere,) * 3,
            scratch_shapes=scratch,
            compiler_params=pltpu.CompilerParams(
                collective_id=0, has_side_effects=True, vmem_limit_bytes=60 * 1024 * 1024
            ),
        )(stored, turned, vertex[None], counts, self_w1, neigh_w1, self_w2, neigh_w2, upstream)
        first = jax.ShapeDtypeStruct((cols, width), f32)
        later = jax.ShapeDtypeStruct((width, width), f32)
        return pl.pallas_call(
            place_kernel,
            out_shape=(jax.ShapeDtypeStruct((graphs, own, width), f32), first, first, later, later),
            in_specs=[anywhere] * 3,
            out_specs=(anywhere,) * 5,
            scratch_shapes=[pltpu.SemaphoreType.DMA((7,))],
        )(*[pltpu.with_memory_space_constraint(one, pltpu.VMEM) for one in held])

    return run


def fitted(mesh):
    node_total, members = mesh.shape["node"], mesh.shape["mp"]

    def run(*args):
        vertex, upstream, stored = args[1], args[8], args[0]
        graphs, own, width = upstream.shape
        fits = (
            members == 4
            and graphs == members
            and node_total == 8
            and own == 128
            and own * members * graphs == vertex.shape[0]
            and args[2].shape[2] % 8 == 0
            and width == 256
            and stored.shape[1] == width
        )
        return (fused(node_total) if fits else body)(*args)

    return run


def solution(mesh):
    placed = (
        P("node", "mp"),
        P("node"),
        P(None, "node", None),
        P(None, "node"),
        P("mp", None),
        P("mp", None),
        P(),
        P(),
        P("node", "mp", None),
    )
    return jax.shard_map(
        fitted(mesh),
        mesh=mesh,
        in_specs=placed,
        out_specs=(P("node", "mp", None), P("mp", None), P("mp", None), P(), P()),
        check_vma=False,
    )
```

```python
import functools
import math

import jax
import jax.numpy as jnp
from jax import lax
from jax.experimental import pallas as pl
from jax.experimental.pallas import tpu as pltpu
from jax.sharding import PartitionSpec as P

epsilon = 1e-05
precise = lax.Precision.HIGHEST


def adjacency(neighbor_ids, row_counts, width):
    row_total = neighbor_ids.shape[0]
    slot_positions = neighbor_ids.shape[1]
    tile_rows = min(128, row_total)
    tiles = row_total // tile_rows
    column_ids = jnp.arange(width, dtype=jnp.int32)
    slot_ids = jnp.arange(slot_positions, dtype=jnp.int32)
    slot_weight = (slot_ids[None, :] < row_counts[:, None]).astype(jnp.float32) / row_counts[
        :, None
    ].astype(jnp.float32)

    def one_tile(packed):
        tile_ids, tile_weight = packed
        hits = (tile_ids[:, :, None] == column_ids[None, None, :]).astype(jnp.float32)
        return jnp.sum(hits * tile_weight[:, :, None], axis=1)

    tiled = lax.map(
        one_tile,
        (
            neighbor_ids.reshape(tiles, tile_rows, slot_positions),
            slot_weight.reshape(tiles, tile_rows, slot_positions),
        ),
    )
    return tiled.reshape(row_total, width)


def normed_parts(pre_act):
    activated = jnp.maximum(pre_act, 0.0)
    inverse = lax.rsqrt(jnp.mean(activated * activated, axis=1, keepdims=True) + epsilon)
    return (activated * inverse, activated, inverse)


def norm_backward(hidden_grad, activated, inverse, pre_act):
    inner_sum = jnp.mean(hidden_grad * activated, axis=1, keepdims=True)
    act_grad = inverse * hidden_grad - activated * (inverse * inverse * inverse) * inner_sum
    return jnp.where(pre_act > 0, act_grad, 0.0)


def body(
    stored_features,
    vertex_row_index,
    neighbors,
    counts,
    self_w1,
    neigh_w1,
    self_w2,
    neigh_w2,
    upstream,
):
    mp_index = lax.axis_index("mp")
    sampled_graphs = upstream.shape[0]
    own_rows = upstream.shape[1]
    row_grand_total = vertex_row_index.shape[0] // sampled_graphs
    column_total = stored_features.shape[1]
    slot_positions = neighbors.shape[2]
    gradient_scale = 1.0 / math.sqrt(row_grand_total * sampled_graphs * lax.axis_size("node"))
    first_row = mp_index * own_rows
    stored_blocks = stored_features.reshape(sampled_graphs, row_grand_total, column_total)
    vertex_blocks = vertex_row_index.reshape(sampled_graphs, row_grand_total)
    neighbor_blocks = jnp.transpose(
        neighbors.reshape(2, sampled_graphs, row_grand_total, slot_positions), (1, 0, 2, 3)
    )
    block_count = jnp.transpose(counts.reshape(2, sampled_graphs, row_grand_total), (1, 0, 2))

    def one_graph(carry, packed):
        store_rows, node_rows, neighbor_ids, row_counts, cotangent = packed
        features = jnp.take(store_rows, node_rows, axis=0)
        adj_zero = adjacency(neighbor_ids[0], row_counts[0], row_grand_total)
        agg_zero = jnp.dot(adj_zero, features, precision=precise)
        own_ids = lax.dynamic_slice_in_dim(neighbor_ids[1], first_row, own_rows, 0)
        own_counts = lax.dynamic_slice_in_dim(row_counts[1], first_row, own_rows, 0)
        adj_own = adjacency(own_ids, own_counts, row_grand_total)
        scaled = cotangent * gradient_scale
        back_neigh = jnp.dot(scaled, neigh_w2.T, precision=precise)
        back_self = jnp.dot(scaled, self_w2.T, precision=precise)
        contrib = lax.dot_general(adj_own, back_neigh, (((0,), (0,)), ((), ())), precision=precise)
        rows_self = features
        rows_neigh = agg_zero
        pre_own = lax.psum_scatter(
            jnp.dot(rows_self, self_w1, precision=precise)
            + jnp.dot(rows_neigh, neigh_w1, precision=precise),
            "mp",
            scatter_dimension=0,
            tiled=True,
        )
        hidden_own, act_own, inverse_own = normed_parts(pre_own)
        hidden_all = lax.all_gather(hidden_own, "mp", axis=0, tiled=True)
        agg_one = jnp.dot(adj_own, hidden_all, precision=precise)
        hidden_grad = lax.psum_scatter(contrib, "mp", scatter_dimension=0, tiled=True) + back_self
        pre_grad = norm_backward(hidden_grad, act_own, inverse_own, pre_own)
        grad_piece = lax.all_gather(pre_grad, "mp", axis=0, tiled=True)
        rows_self = features
        rows_neigh = agg_zero
        step_self1 = carry[0] + jnp.dot(rows_self.T, grad_piece, precision=precise)
        step_neigh1 = carry[1] + jnp.dot(rows_neigh.T, grad_piece, precision=precise)
        graph_out = jnp.dot(hidden_own, self_w2, precision=precise) + jnp.dot(
            agg_one, neigh_w2, precision=precise
        )
        step_self2 = carry[2] + jnp.dot(hidden_own.T, scaled, precision=precise)
        step_neigh2 = carry[3] + jnp.dot(agg_one.T, scaled, precision=precise)
        return ((step_self1, step_neigh1, step_self2, step_neigh2), graph_out)

    zero_first = jnp.zeros(self_w1.shape, jnp.float32)
    zero_second = jnp.zeros(self_w2.shape, jnp.float32)
    totals, layer_out = lax.scan(
        one_graph,
        (zero_first, zero_first, zero_second, zero_second),
        (stored_blocks, vertex_blocks, neighbor_blocks, block_count, upstream),
    )
    grad_self1, grad_neigh1, grad_self2, grad_neigh2 = totals
    grad_self1, grad_neigh1, grad_self2, grad_neigh2 = lax.psum(
        (grad_self1, grad_neigh1, grad_self2, grad_neigh2), "node"
    )
    grad_self2, grad_neigh2 = lax.psum((grad_self2, grad_neigh2), "mp")
    return (layer_out, grad_self1, grad_neigh1, grad_self2, grad_neigh2)


f32 = jnp.float32
bf16 = jnp.bfloat16


def halves(value):
    high = value.astype(bf16)
    return high, (value - high.astype(f32)).astype(bf16)


def thirds(value):
    high = value.astype(bf16)
    rest = value - high.astype(f32)
    middle = rest.astype(bf16)
    return high, middle, (rest - middle.astype(f32)).astype(bf16)


def mul(left, right, dims=((1,), (0,))):
    return lax.dot_general(left, right, (dims, ((), ())), preferred_element_type=f32)


def mul3(left, right, dims=((1,), (0,))):
    return (
        mul(left[0], right[0], dims) + mul(left[1], right[0], dims) + mul(left[0], right[1], dims)
    )


def mul6(left, right):
    small = mul(left[2], right[0]) + mul(left[0], right[2]) + mul(left[1], right[1])
    return mul(left[0], right[0]) + (mul(left[0], right[1]) + mul(left[1], right[0]) + small)


def fused_kernel(
    slots,
    scale,
    store_h,
    nbr_h,
    vertex_h,
    counts_h,
    s1_h,
    n1_h,
    s2_h,
    n2_h,
    up_h,
    out_ref,
    g1_ref,
    g2_ref,
    store,
    nbr,
    vertex,
    counts,
    w1f,
    w2f,
    upg,
    grid,
    adj_even,
    adj_odd,
    hot_even,
    hot_odd,
    rec_t,
    rec,
    part,
    pin,
    psum,
    near,
    far,
    pg,
    xh,
    xl,
    xt,
    wh,
    wl,
    wt,
    hid,
    hg,
    g1acc,
    g2acc,
    g2p,
    outg,
    xin,
    half,
    zin,
    mid,
    xin2,
    half2,
    zin2,
    mid2,
    yin2,
    load_sems,
    send_sems,
    recv_sems,
):
    rows, width = upg.shape
    own = up_h.shape[1]
    cols = store_h.shape[1]
    node = lax.axis_index("node")
    member = lax.axis_index("mp")
    zc, xc = node // 2, node % 2
    yc, cc = member // 2, member % 2
    partner = yc * 2 + (1 - cc)
    across = (1 - yc) * 2 + cc
    diagonal = (1 - yc) * 2 + (1 - cc)
    peers = (partner, across, diagonal)
    x_peer = zc * 2 + (1 - xc)
    z_pair = (zc + 1 - 2 * (zc % 2)) * 2 + xc
    z_mate = (3 - zc) * 2 + xc
    inner = jnp.logical_or(zc == 1, zc == 2)
    outer = jnp.logical_or(zc == 0, zc == 3)
    graphs = ((1 - yc) * 2, (1 - yc) * 2 + 1, partner, member)

    def target(node_id, member_id):
        return dict(device_id=(node_id, member_id), device_id_type=pl.DeviceIdType.MESH)

    sending, receiving = {}, {}

    def place(table, key):
        key = ("own", len(table)) if key is None else key
        return table.setdefault(key, len(table))

    def copy(source, dest, node_id, member_id, send=None, recv=None, slot=None):
        return pltpu.make_async_remote_copy(
            src_ref=source,
            dst_ref=dest,
            send_sem=send_sems.at[place(sending, send)],
            recv_sem=recv_sems.at[place(receiving, recv) if slot is None else slot],
            **target(node_id, member_id),
        )

    def sent(key, ref):
        copy(ref, ref, node, partner, send=key, recv="out").wait_send()

    def received(key, ref):
        copy(ref, ref, node, partner, send="out", recv=key).wait_recv()

    def block(index, size):
        return pl.ds(pl.multiple_of(index * size, size), size)

    loading = {}

    def local(source, dest, key=None):
        return pltpu.make_async_copy(source, dest, load_sems.at[place(loading, key)])

    def load(source, dest, key=None):
        one = local(source, dest, key)
        one.start()
        return one

    barrier = pltpu.get_barrier_semaphore()
    for p in peers:
        pl.semaphore_signal(barrier, inc=1, **target(node, p))
    pl.semaphore_signal(barrier, inc=1, **target(x_peer, member))
    pl.semaphore_signal(barrier, inc=1, **target(z_pair, member))
    pl.semaphore_signal(barrier, inc=1, **target(z_mate, member))

    id_loads = [load(nbr_h, nbr), load(vertex_h, vertex), load(counts_h, counts)]
    store_loads = [load(store_h.at[block(graphs[0], rows)], store.at[0])]
    load(s1_h, w1f.at[0], "w1")
    load(n1_h, w1f.at[1], "w1")
    for s in range(1, 4):
        store_loads.append(load(store_h.at[block(graphs[s], rows)], store.at[s]))
    load(s2_h, w2f.at[0], "w2")
    load(n2_h, w2f.at[1], "w2")
    up_load = load(up_h.at[member], upg.at[block(member, own)])

    packs = rows // 16
    middle = rows // 2
    spot = lax.broadcasted_iota(jnp.int32, (packs, 16, 128), 0) * 16
    spot = spot + lax.broadcasted_iota(jnp.int32, (packs, 16, 128), 1) - middle
    grid[...] = spot.astype(f32).astype(bf16)
    rec_t[...] = jnp.ones_like(rec_t)
    one_b, none_b = jnp.ones((), bf16), jnp.zeros((), bf16)
    slot = lax.broadcasted_iota(jnp.int32, (slots, 128), 0)
    group = 8

    def pieces(adj, hot, layer, graph):
        todo = []
        for c in range(rows // 128):
            lane = pl.ds(pl.multiple_of(graph * rows + c * 128, 128), 128)
            to = pl.ds(c * 128, 128)

            def prepare(lane=lane):
                used = slot < counts[layer : layer + 1, lane]
                ids = jnp.where(used, nbr[layer, :, lane], 4 * rows)
                ids = (ids - middle).astype(f32)
                keys = [
                    jnp.broadcast_to(ids[k : k + 1], (16, 128)).astype(bf16) for k in range(slots)
                ]
                if hot is None:
                    return keys
                at = (vertex[0:1, lane] - middle).astype(f32)
                return keys + [jnp.broadcast_to(at, (16, 128)).astype(bf16)]

            kept = []
            for j in range(packs // group):

                def unit(j=j, prepare=prepare, kept=kept, to=to):
                    if not kept:
                        kept.append(prepare())
                    keys = kept[0]
                    span = pl.ds(j * group, group)
                    lanes = grid[span]
                    total = jnp.where(keys[0][None] == lanes, one_b, none_b)
                    for k in range(1, slots):
                        total = total + jnp.where(keys[k][None] == lanes, one_b, none_b)
                    adj[span, :, to] = total
                    if hot is not None:
                        hot[span, :, to] = jnp.where(keys[slots][None] == lanes, one_b, none_b)

                todo.append(unit)
        return todo

    def square(ref):
        return ref[...].reshape(rows, rows)

    tn = ((0,), (0,))
    nt = ((1,), (1,))

    with jax.named_scope("barrier"):
        pl.semaphore_wait(barrier, 6)
    up_copies = [
        copy(up_h.at[p], upg.at[block(member, own)], node, p, send="up", recv="up") for p in peers
    ]
    three = pl.ds(0, 3 * own)
    for one in up_copies[1:] + up_copies[:1]:
        one.start()
    for one in id_loads:
        one.wait()
    with jax.named_scope("first_build"):
        for unit in pieces(adj_even, hot_even, 0, graphs[0]):
            unit()
        for s in range(4):
            rec_t[s : s + 1] = 1.0 / counts[0:1, block(graphs[s], rows)].astype(f32)
        rec_t[4:5] = 1.0 / counts[1:2, block(member, rows)].astype(f32)
        rec[...] = jnp.transpose(rec_t[...])

    local(w1f, w1f, "w1").wait()
    wh[:cols], wl[:cols], wt[:cols] = thirds(w1f[0])
    wh[cols:], wl[cols:], wt[cols:] = thirds(w1f[1])

    side = rows // 2
    pin_copies = [
        copy(part.at[s, block(1 - cc, side)], pin.at[s], node, partner, send="pin")
        for s in range(2)
    ]
    far_slot = place(receiving, "far0")
    place(receiving, "far1")
    far_copies = [
        copy(
            psum.at[s],
            far.at[block(cc, side)],
            node,
            (1 - yc) * 2 + s,
            send="far",
            slot=far_slot + cc,
        )
        for s in range(2)
    ]
    far_waits = [
        copy(
            psum.at[i],
            far.at[pl.ds(i * side, side)],
            node,
            across,
            send="far",
            recv=f"far{i}",
        )
        for i in range(2)
    ]
    near_copy = copy(part.at[2], near, node, partner)

    def pass_on(s):
        pin_copies[s].wait_recv()
        psum[s] = part[s, block(cc, side)] + pin[s]
        far_copies[s].start()

    tiles = rows // 128
    for s in range(4):
        adj, hot = (adj_even, hot_even) if s % 2 == 0 else (adj_odd, hot_odd)
        adj_next, hot_next = (adj_odd, hot_odd) if s % 2 == 0 else (adj_even, hot_even)
        with jax.named_scope(f"graph{s}"):
            store_loads[s].wait()
            if s < 3:
                todo = pieces(adj_next, hot_next, 0, graphs[s + 1])
            else:
                todo = pieces(adj_next, None, 1, member)
            per = -(-len(todo) // (2 * tiles))

            def some():
                for _ in range(per):
                    if todo:
                        todo.pop(0)()

            kept = jnp.concatenate(thirds(store[s]), axis=1)
            for t in range(tiles):
                span = pl.ds(t * 128, 128)
                pick = hot[:, :, span].reshape(rows, 128)
                found = mul(pick, kept, tn)
                xh[s, span, :cols] = found[:, :cols].astype(bf16)
                xl[s, span, :cols] = found[:, cols : 2 * cols].astype(bf16)
                xt[span, :cols] = found[:, 2 * cols :].astype(bf16)
                some()
                if t == 2 and (s == 1 or s == 2):
                    pass_on(s - 1)
            source = jnp.concatenate([xt[:, :cols], xl[s, :, :cols], xh[s, :, :cols]], axis=1)
            for t in range(tiles):
                span = pl.ds(t * 128, 128)
                pick = adj[:, :, span].reshape(rows, 128)
                agg = mul(pick, source, tn)
                agg = agg[:, :cols] + agg[:, cols : 2 * cols] + agg[:, 2 * cols :]
                ah, al, at = thirds(agg * rec[span, s : s + 1])
                xh[s, span, cols:] = ah
                xl[s, span, cols:] = al
                xt[span, cols:] = at
                part[s, span] = mul6(
                    (xh[s, span], xl[s, span], xt[span]), (wh[...], wl[...], wt[...])
                )
                some()
        if s < 2:
            pin_copies[s].start()
        if s == 2:
            near_copy.start()

    shrink = rec[:, 4:5]
    with jax.named_scope("back"):
        local(w2f, w2f, "w2").wait()
        up_load.wait()
        received("up", upg.at[three])
        scaled = halves(upg[...] * scale)
        w2s = halves(w2f[0])
        w2n = halves(w2f[1])
        back = halves(mul3(scaled, w2n, nt) * shrink)
        adj = square(adj_even)
        hg[...] = mul3(scaled, w2s, nt) + mul(adj, back[0]) + mul(adj, back[1])

    wing = width // 2
    pg_partner = copy(pg.at[3], pg.at[2], node, partner)
    halls = [(h, pl.ds(r * side, side)) for h in range(2) for r in range(2)]
    pg_across = [copy(pg.at[3, h, r], pg.at[cc, h, r], node, across, send="pg") for h, r in halls]
    pg_forward = [
        copy(pg.at[cc, h, r], pg.at[cc, h, r], node, partner, send="onward", recv=("onward", h))
        for h, r in halls
    ]
    with jax.named_scope("norm"):
        near_copy.wait_recv()
        for i in range(2):
            far_waits[i].wait_recv()
            span = pl.ds(i * side, side)
            pre = part[3, span] + near[span] + far[span]
            hidden, activated, inverse = normed_parts(pre)
            hid[span] = hidden
            gradient = norm_backward(hg[span], activated, inverse, pre)
            pg[3, 0, span] = gradient[:, :wing]
            pg[3, 1, span] = gradient[:, wing:]
            pg_across[i].start()
        pg_across[2].start()
        pg_across[3].start()
        pg_partner.start()

    with jax.named_scope("second_gradients"):
        hidden = halves(hid[...])
        adj = square(adj_even)
        agg_one = halves((mul(adj, hidden[0], tn) + mul(adj, hidden[1], tn)) * shrink)
        scaled = halves(upg[...] * scale)
        g2acc[0] = mul3(hidden, scaled, tn)
        g2acc[1] = mul3(agg_one, scaled, tn)
        g2_partner = copy(g2acc, g2p, node, partner)
        lead = cc == 1
        helper = cc == 0

        @pl.when(helper)
        def _():
            g2_partner.start()

    with jax.named_scope("output"):
        w2s = halves(w2f[0])
        w2n = halves(w2f[1])
        outg[...] = mul3(hidden, w2s) + mul3(agg_one, w2n)
    out_copies = [
        copy(outg.at[block(p, own)], out_ref.at[member], node, p, send="out", recv="out")
        for p in peers
    ]
    out_here = load(outg.at[block(member, own)], out_ref.at[member])

    def reduction(full, base, size, result, to, bufs, held, tag):
        size = size // 2
        x_in, x_sum, z_in, m_in = bufs[:4]
        away = pl.ds(pl.multiple_of(base + (1 - xc) * size, size), size)
        home = pl.ds(pl.multiple_of(base + xc * size, size), size)
        mine = pl.ds(pl.multiple_of(to + xc * size, size), size)
        name, i = tag
        one = dict(
            full=full,
            home=home,
            mine=mine,
            result=result,
            bufs=bufs,
            x=copy(full.at[away], x_in, x_peer, member, send=(name, "x")),
            z=copy(x_sum, z_in, z_pair, member, send=(name, "z"), recv=(name, "z", i)),
            m=copy(x_sum, m_in, z_mate, member, send=(name, "z")),
            o=copy(held, result.at[mine], z_pair, member, send=(name, "o"), recv=(name, "z", i)),
            keep=local(held, result.at[mine], name),
        )
        for key, source in (("e", held), ("relay", result.at[mine])):
            one[key] = copy(
                source, result.at[mine], x_peer, member, send=(name, "e"), recv=(name, "e")
            )
        return one

    chunk = 128
    chunks = g1acc.shape[1] // chunk
    sets = []
    for h in range(2):
        for e in range(chunks):
            bufs = [b.at[h * chunks + e] for b in (xin, half, zin, mid)]
            at = e * chunk
            tag = (1, h * chunks + e)
            sets.append(
                reduction(g1acc.at[h], at, chunk, g1_ref.at[h], at, bufs, bufs[3], tag)
            )
    pairs = []
    for i in range(2):
        bufs = [b.at[i] for b in (xin2, half2, zin2, mid2)]
        pairs.append(reduction(g2acc.at[i], 0, width, g2_ref.at[yc], 0, bufs, yin2, (2, i)))
    y_copy = copy(mid2.at[1 - yc], yin2, node, across)
    slabs = [block(xc, width // 2), block(1 - xc, width // 2)]

    def g2_copy(source, a, r, member_id, recv):
        return copy(source, g2_ref.at[a, r], node, member_id, send="g2", recv=recv)

    g2_near = copy(g2_ref.at[yc], g2_ref.at[yc], node, partner, recv="near")
    g2_far = [g2_copy(g2_ref.at[yc, r], yc, r, across, ("g2", i)) for i, r in enumerate(slabs)]
    g2_first = g2_copy(yin2, yc, slabs[0], across, ("g2", 0))
    g2_onward = [g2_copy(g2_ref.at[1 - yc, r], 1 - yc, r, partner, "near") for r in slabs]

    def stage_x(one):
        x_in, x_sum = one["bufs"][:2]
        one["x"].wait_recv()
        x_sum[...] = one["full"][one["home"]] + x_in[...]

        @pl.when(outer)
        def _():
            one["z"].start()

    def stage_z(one):
        @pl.when(inner)
        def _():
            x_sum, z_in = one["bufs"][1:3]
            one["z"].wait_recv()
            x_sum[...] = x_sum[...] + z_in[...]
            one["m"].start()

    def spread(one, held):
        one["o"].start()
        one["e"].start()
        one["keep"].start()

    def stage_m(one):
        @pl.when(inner)
        def _():
            x_sum, z_in, m_in = one["bufs"][1:4]
            one["m"].wait_recv()
            m_in[...] = x_sum[...] + m_in[...]
            if one is pairs[1]:
                y_copy.start()
            elif one is not pairs[0]:
                spread(one, m_in)

    def stage_y(one):
        @pl.when(inner)
        def _():
            y_copy.wait_recv()
            yin2[...] = mid2[yc] + yin2[...]
            spread(one, yin2)
            g2_first.start()

    def stage_o(one):
        @pl.when(outer)
        def _():
            one["o"].wait_recv()
            one["relay"].start()
            if one is pairs[0]:
                g2_far[0].start()

    def stage_e(one):
        one["e"].wait_recv()

    def g2_out(role):
        @pl.when(jnp.logical_and(role, lead))
        def _():
            pairs[0]["e"].wait_recv()
            if role is inner:
                pairs[0]["keep"].wait()
            g2_far[1].start()
            g2_near.start()

    def g2_on(i):
        @pl.when(lead)
        def _():
            g2_far[i].wait_recv()
            g2_onward[i].start()

    def both(k):
        return xh[k], xl[k]

    @pl.when(lead)
    def _():
        g2_partner.wait_recv()
        g2acc[...] = g2acc[...] + g2p[...]
        for one in pairs:
            one["x"].start()

    with jax.named_scope("early_gradients"):
        for h in range(2):
            g1acc[h] = mul3(both(3), halves(pg[3, h]), tn)
        pg_partner.wait_recv()
        for h in range(2):
            g1acc[h] += mul3(both(2), halves(pg[2, h]), tn)

    def arrive(h):
        with jax.named_scope(f"across_wait{h}"):
            for i in (2 * h, 2 * h + 1):
                pg_across[i].wait_recv()
                pg_forward[i].start()

    def late(h):
        with jax.named_scope(f"late_gradients{h}"):
            g1acc[h] += mul3(both(cc), halves(pg[cc, h]), tn)

    def forwarded(h):
        with jax.named_scope(f"forward_wait{h}"):
            received(("onward", h), pg.at[1 - cc, h])

    def last(h, c):
        other = 1 - cc
        with jax.named_scope(f"last_gradients{h}{c}"):
            span = pl.ds(c * chunk, chunk)
            picked = (xh[other, :, span], xl[other, :, span])
            g1acc[h, span] += mul3(picked, halves(pg[other, h]), tn)
            sets[h * chunks + c]["x"].start()

    named = dict(X=stage_x, Z=stage_z, M=stage_m, O=stage_o, E=stage_e, Y=stage_y)

    def go(*words):
        for word in words:
            with jax.named_scope(word):
                if word[1] == "g":
                    pl.when(lead)(functools.partial(named[word[0]], pairs[int(word[2])]))
                else:
                    named[word[0]](sets[int(word[1])])

    go("Xg0", "Xg1")
    arrive(0)
    late(0)
    forwarded(0)
    for c in range(chunks):
        last(0, c)
    go("Zg0", "Zg1")
    arrive(1)
    late(1)
    forwarded(1)
    for c in range(chunks):
        last(1, c)
    go("X0", "X1", "X2", "X3", "Mg0", "Mg1")
    for one in out_copies[1:] + out_copies[:1]:
        one.start()
    go("X4", "Z0", "X5", "Z1", "X6", "Z2", "X7", "Z3", "Z4", "Yg0", "M0", "Z5", "M1", "Z6", "M2", "Z7", "M3", "M4")
    g2_out(inner)
    go("M5", "M6", "M7")
    go("Og0", "O0", "O1", "O2", "O3", "O4")
    g2_out(outer)
    go("O5", "O6", "O7")
    g2_on(0)
    g2_on(1)
    with jax.named_scope("ends"):
        received((1, "e"), mid)
    with jax.named_scope("g2_last"):
        @pl.when(helper)
        def _():
            received("near", g2acc)

    with jax.named_scope("drain"):
        sent("up", upg.at[three])
        sent("pin", psum)
        sent("far", psum)
        near_copy.wait_send()
        pg_partner.wait_send()
        sent("pg", pg.at[3])
        sent("onward", pg.at[0])
        sent("out", outg.at[three])
        received("out", outg.at[three])
        out_here.wait()
        sent((1, "x"), xin)
        sent((1, "z"), zin)
        sent((1, "e"), mid)

        @pl.when(helper)
        def _():
            g2_partner.wait_send()

        @pl.when(lead)
        def _():
            sent("g2", g2acc)
            g2_near.wait_send()
            sent((2, "x"), xin2)
            sent((2, "z"), zin2)
            sent((2, "e"), yin2)

        @pl.when(inner)
        def _():
            sent((1, "o"), mid)
            local(mid, mid, 1).wait()

        @pl.when(jnp.logical_and(inner, lead))
        def _():
            sent((2, "o"), yin2)
            y_copy.wait_send()


def place_kernel(out_ref, g1_ref, g2_ref, out, gs1, gn1, gs2, gn2, sems):
    cols, wing = gs1.shape[0], g1_ref.shape[2]
    pairs = [(out_ref, out), (g2_ref.at[0], gs2), (g2_ref.at[1], gn2)]
    for h in range(2):
        span = pl.ds(h * wing, wing)
        pairs.append((g1_ref.at[h, pl.ds(0, cols)], gs1.at[:, span]))
        pairs.append((g1_ref.at[h, pl.ds(cols, cols)], gn1.at[:, span]))
    copies = [pltpu.make_async_copy(a, b, sems.at[i]) for i, (a, b) in enumerate(pairs)]
    for one in copies:
        one.start()
    for one in copies:
        one.wait()


def fused(mesh_node):
    def run(stored, vertex, neighbors, counts, self_w1, neigh_w1, self_w2, neigh_w2, upstream):
        graphs, own, width = upstream.shape
        rows = vertex.shape[0] // graphs
        slots = neighbors.shape[2]
        cols = stored.shape[1]
        total = vertex.shape[0]
        turned = jnp.transpose(neighbors, (0, 2, 1))
        scale = 1.0 / math.sqrt(total * mesh_node)
        wide = 2 * cols
        wing = width // 2
        chunks = 2 * (wide // 128)
        vm = pltpu.VMEM
        scratch = [
            vm((4, rows, cols), f32),
            vm(turned.shape, jnp.int32),
            vm((1, total), jnp.int32),
            vm(counts.shape, jnp.int32),
            vm((2, cols, width), f32),
            vm((2, width, width), f32),
            vm((rows, width), f32),
            vm((rows // 16, 16, 128), bf16),
            vm((rows // 16, 16, rows), bf16),
            vm((rows // 16, 16, rows), bf16),
            vm((rows // 16, 16, rows), bf16),
            vm((rows // 16, 16, rows), bf16),
            vm((128, rows), f32),
            vm((rows, 128), f32),
            vm((4, rows, width), f32),
            vm((2, rows // 2, width), f32),
            vm((2, rows // 2, width), f32),
            vm((rows, width), f32),
            vm((rows, width), f32),
            vm((4, 2, rows, wing), f32),
            vm((4, rows, wide), bf16),
            vm((4, rows, wide), bf16),
            vm((rows, wide), bf16),
            vm((wide, width), bf16),
            vm((wide, width), bf16),
            vm((wide, width), bf16),
            vm((rows, width), f32),
            vm((rows, width), f32),
            vm((2, wide, wing), f32),
            vm((2, width, width), f32),
            vm((2, width, width), f32),
            vm((rows, width), f32),
        ]
        scratch += [vm((chunks, 64, wing), f32) for _ in range(4)]
        scratch += [vm((2, width // 2, width), f32) for _ in range(4)]
        scratch += [vm((width // 2, width), f32)]
        scratch += [
            pltpu.SemaphoreType.DMA((13,)),
            pltpu.SemaphoreType.DMA((20,)),
            pltpu.SemaphoreType.DMA((51,)),
        ]
        anywhere = pl.BlockSpec(memory_space=pl.ANY)
        held = pl.pallas_call(
            functools.partial(fused_kernel, slots, scale),
            out_shape=(
                pltpu.VMEM((graphs, own, width), f32),
                pltpu.VMEM((2, wide, wing), f32),
                pltpu.VMEM((2, width, width), f32),
            ),
            in_specs=[anywhere] * 9,
            out_specs=(anywhere,) * 3,
            scratch_shapes=scratch,
            compiler_params=pltpu.CompilerParams(
                collective_id=0, has_side_effects=True, vmem_limit_bytes=60 * 1024 * 1024
            ),
        )(stored, turned, vertex[None], counts, self_w1, neigh_w1, self_w2, neigh_w2, upstream)
        first = jax.ShapeDtypeStruct((cols, width), f32)
        later = jax.ShapeDtypeStruct((width, width), f32)
        return pl.pallas_call(
            place_kernel,
            out_shape=(jax.ShapeDtypeStruct((graphs, own, width), f32), first, first, later, later),
            in_specs=[anywhere] * 3,
            out_specs=(anywhere,) * 5,
            scratch_shapes=[pltpu.SemaphoreType.DMA((7,))],
        )(*[pltpu.with_memory_space_constraint(one, pltpu.VMEM) for one in held])

    return run


def fitted(mesh):
    node_total, members = mesh.shape["node"], mesh.shape["mp"]

    def run(*args):
        vertex, upstream, stored = args[1], args[8], args[0]
        graphs, own, width = upstream.shape
        fits = (
            members == 4
            and graphs == members
            and node_total == 8
            and own == 128
            and own * members * graphs == vertex.shape[0]
            and args[2].shape[2] % 8 == 0
            and width == 256
            and stored.shape[1] == width
        )
        return (fused(node_total) if fits else body)(*args)

    return run


def solution(mesh):
    placed = (
        P("node", "mp"),
        P("node"),
        P(None, "node", None),
        P(None, "node"),
        P("mp", None),
        P("mp", None),
        P(),
        P(),
        P("node", "mp", None),
    )
    return jax.shard_map(
        fitted(mesh),
        mesh=mesh,
        in_specs=placed,
        out_specs=(P("node", "mp", None), P("mp", None), P("mp", None), P(), P()),
        check_vma=False,
    )
```
